32 devices in a mesh: groups: 2 (over y), tensor: 4 (over z), section: 2 (over x), seq: 2 (over core).
Axes of the slice: x: 2, y: 2, z: 4, core: 2. Of those that a mesh axis runs over, the one named last changes fastest.
Arguments:
- token_ids: int32 [4, 96], P('groups'), parts along dimension 0, may hold values from 0 to 511
- leading_span_index: int32 [2], P('groups'), parts along dimension 0, may hold values from 8 to 4103
- embed_table: float32 [512, 8192], P(None, 'tensor'), may hold values from -6 to 6
- norm_gain: float32 [2, 8192], P('section', 'tensor'), may hold values from 0.25 to 1.75
- decay_rates: float32 [2, 16, 8192], P('section', None, 'tensor'), may hold values from 0.0002 to 0.03
- residues: float32 [2, 16, 8192], P('section', None, 'tensor'), may hold values from -0.12 to 0.12
- history: float32 [2, 8, 192, 8192], P('section', 'seq', 'groups', 'tensor'), parts along dimension 2, may hold values from -6 to 6
- mix_weight: bfloat16 [2, 8192, 8192], P('section', None, ('tensor', 'seq')), may hold values from -0.0625 to 0.0625
Outputs:
- section_out: float32 [2, 2, 192, 8192], P('section', None, 'groups', ('tensor', 'seq')), parts along dimension 2
The draws below stay inside these ranges and needn't reach their ends.
There are 2 independent parts, one for each index of `groups`. The reference program is written for one: setup_inputs(seed, part) draws one part's arguments, and reference() takes and returns one part's arrays. A program takes and returns all parts, laid end to end along the dimension named above; an argument that names none is the same for every part. Nothing has to cross between parts.
Inputs may be any that keep to these rules, and one draw needn't show every extreme that they name: `leading_span_index`: index of the first span of the run; the span before it is the newest one in history.
All inputs are finite; a program needn't handle non-finite values.
Results may differ from the reference program's by a relative error of at most 0.0036.
Values may be sent and summed in bfloat16 or wider, within the bound.
No kernel may reach another device: no remote copies, remote signals or barrier semaphores. Data moves between devices by JAX's collectives and lax.ppermute only.
A program may use at most 128 MiB of HBM per device.

```python
import math
import jax
import jax.numpy as jnp
from jax import lax

MODEL_WIDTH = 8192
VOCAB = 512
MODES = 16
SPANS = 2
SPAN_TOKENS = 96
HISTORY_SPANS = 8
SECTION_LAYERS = 2


def place_ends(array, stream_key, low, top_value):
    spot = [jax.random.randint(jax.random.fold_in(stream_key, axis), (), 0, length) for axis, length in enumerate(array.shape)]
    widest = array.shape.index(max(array.shape))
    beside = spot[:widest] + [(spot[widest] + 1) % array.shape[widest]] + spot[widest + 1:]
    return array.at[tuple(spot)].set(low).at[tuple(beside)].set(top_value)


def shard_levels(key, extent, cuts, low, high):
    level = 1.0
    for axis_at, parts in cuts:
        steps = jax.random.uniform(jax.random.fold_in(jax.random.fold_in(key, 6), axis_at), (parts,), jnp.float32, low / len(cuts), high / len(cuts))
        level = level * jnp.repeat(jnp.exp(steps), extent[axis_at] // parts).reshape((-1,) + (1,) * (len(extent) - 1 - axis_at))
    return level


def noise(key, shape, deviation, bound, shards=(), dtype=jnp.bfloat16):
    entries = jax.random.normal(key, shape, jnp.float32) * deviation
    if len(shards) > 0:
        entries = shard_levels(key, shape, shards, -0.22, 0.18) * entries
    return jnp.clip(entries, min=-bound, max=bound).astype(dtype)


def setup_inputs(seed: int = 0, part: int = 0) -> dict:
    arg_keys = jax.random.split(jax.random.key(seed), 9)
    own_keys = jax.random.split(jax.random.fold_in(arg_keys[8], part), 9)
    token_ids = place_ends(jax.random.randint(own_keys[0], (SPANS, SPAN_TOKENS), 0, VOCAB), jax.random.fold_in(own_keys[0], 1), 0, VOCAB - 1).astype(jnp.int32)
    leading_span_index = jax.random.randint(own_keys[1], (1,), HISTORY_SPANS, HISTORY_SPANS + 4096).astype(jnp.int32)
    embed_table = noise(arg_keys[2], (VOCAB, MODEL_WIDTH), 1.0, 6.0, ((1, 4),), jnp.float32)
    norm_gain = jnp.clip(1.0 + 0.15 * jax.random.normal(arg_keys[3], (SECTION_LAYERS, MODEL_WIDTH), jnp.float32), 0.25, 1.75)
    decay_rates = jnp.clip(jnp.exp(math.log(0.03) - 5.0106353 * jax.random.uniform(arg_keys[4], (SECTION_LAYERS, MODES, MODEL_WIDTH), jnp.float32) ** shard_levels(arg_keys[4], (SECTION_LAYERS, MODES, MODEL_WIDTH), ((0, 2), (2, 4)), -0.2, 0.2)), 0.0002, 0.03)
    residues = noise(arg_keys[5], (SECTION_LAYERS, MODES, MODEL_WIDTH), 0.02, 0.12, ((0, 2), (2, 4)), jnp.float32)
    history = noise(own_keys[6], (SECTION_LAYERS, HISTORY_SPANS, SPAN_TOKENS, MODEL_WIDTH), 1.0, 6.0, ((0, 2), (1, 2), (3, 4)), jnp.float32)
    mix_weight = noise(arg_keys[7], (SECTION_LAYERS, MODEL_WIDTH, MODEL_WIDTH), MODEL_WIDTH ** -0.5, 0.0625, ((0, 2), (2, 8)))
    return dict(token_ids=token_ids, leading_span_index=leading_span_index, embed_table=embed_table, norm_gain=norm_gain, decay_rates=decay_rates, residues=residues, history=history, mix_weight=mix_weight)


def build_taps(rates, weights, count):
    lag_pos = jnp.arange(count).astype(jnp.float32)
    taps_sum = jnp.zeros((count, rates.shape[1]), jnp.float32)
    for mode_num in range(rates.shape[0]):
        taps_sum = taps_sum + weights[mode_num][None, :] * jnp.exp(-rates[mode_num][None, :] * lag_pos[:, None])
    return taps_sum

def causal_conv(signal, taps_all):
    count = signal.shape[0]
    length = 2 * count
    spectrum = jnp.fft.rfft(signal, n=length, axis=0) * jnp.fft.rfft(taps_all, n=length, axis=0)
    return jnp.fft.irfft(spectrum, n=length, axis=0)[:count].astype(jnp.float32)

def reference(token_ids, leading_span_index, embed_table, norm_gain, decay_rates, residues, history, mix_weight):
    slot_total = history.shape[1]
    row_count = token_ids.shape[1]
    width = embed_table.shape[1]
    first_span = leading_span_index[0]
    slot_ages = jnp.arange(slot_total, 0, -1).astype(jnp.int32)
    slot_order = ((first_span - slot_ages) % slot_total).astype(jnp.int32)
    current = jnp.take(embed_table, token_ids, axis=0)
    results = []
    for section_num in range(SECTION_LAYERS):
        mean_sq = lax.optimization_barrier(jnp.mean(current * current, axis=-1))
        normed = current * lax.rsqrt(mean_sq + 1e-05)[..., None] * norm_gain[section_num][None, None, :]
        past = jnp.take(history[section_num], slot_order, axis=0).reshape(slot_total * row_count, width)
        sequence_a = jnp.concatenate([past, normed[0]], axis=0)
        sequence_b = jnp.concatenate([past[row_count:], normed[0], normed[1]], axis=0)
        count = sequence_a.shape[0]
        taps_all = build_taps(decay_rates[section_num], residues[section_num], count)
        conv_a = causal_conv(sequence_a, taps_all)[count - row_count:]
        conv_b = causal_conv(sequence_b, taps_all)[count - row_count:]
        conv_out = jnp.stack([conv_a, conv_b])
        gated = (normed * conv_out).astype(jnp.bfloat16)
        mixed = jnp.dot(gated.reshape(-1, width), mix_weight[section_num], preferred_element_type=jnp.float32)
        current = current + mixed.reshape(current.shape)
        results.append(current)
    return jnp.stack(results)
```

```python
import functools

import jax
import jax.numpy as jnp
from jax import lax
from jax.experimental import pallas as pl
from jax.experimental.pallas import tpu as pltpu
from jax.sharding import PartitionSpec as P

epsilon = 1e-05
highest = lax.Precision.HIGHEST
LANES = 128
SUB = 8
f32 = jnp.float32
VMEM_BYTES = 24 << 20


def params(**more):
    return pltpu.CompilerParams(vmem_limit_bytes=VMEM_BYTES, **more)


def cost(flops, moved):
    return pl.CostEstimate(flops=int(flops), bytes_accessed=int(moved), transcendentals=0)


def row_sums(squares):
    ones = jnp.ones((SUB, squares.shape[1]), f32)
    return lax.dot_general(
        ones, squares, (((1,), (1,)), ((), ())), precision=highest, preferred_element_type=f32
    )


def lane_tiles_squared(block):
    total = block[:, :LANES] * block[:, :LANES]
    for start in range(LANES, block.shape[1], LANES):
        piece = block[:, start : start + LANES]
        total = total + piece * piece
    return total


def embed_body(ids, meta, table, x_out, sums_out, rows_buf, sem):
    count = rows_buf.shape[0]
    half = x_out.shape[1]

    def fetch(i, carry):
        pltpu.make_async_copy(
            table.at[pl.ds(ids[i], 1), :], rows_buf.at[pl.ds(i, 1), :], sem
        ).start()
        return carry

    lax.fori_loop(0, count, fetch, 0, unroll=8)
    pltpu.make_async_copy(table.at[pl.ds(0, count), :], rows_buf, sem).wait()
    sums_out[...] = row_sums(lane_tiles_squared(rows_buf[...]))
    for part in range(rows_buf.shape[1] // half):

        @pl.when(meta[1] == part)
        def _():
            x_out[...] = rows_buf[:, part * half : (part + 1) * half]


def embed_rows(ids, meta, table, half):
    count = ids.shape[0]
    width = table.shape[1]
    return pl.pallas_call(
        embed_body,
        out_shape=(
            jax.ShapeDtypeStruct((count, half), f32),
            jax.ShapeDtypeStruct((SUB, count), f32),
        ),
        grid_spec=pltpu.PrefetchScalarGridSpec(
            num_scalar_prefetch=2,
            grid=(1,),
            in_specs=[pl.BlockSpec(memory_space=pl.ANY)],
            out_specs=(
                pl.BlockSpec((count, half), lambda i, *_: (0, 0)),
                pl.BlockSpec((SUB, count), lambda i, *_: (0, 0)),
            ),
            scratch_shapes=[pltpu.VMEM((count, width), f32), pltpu.SemaphoreType.DMA],
        ),
        compiler_params=params(),
        cost_estimate=cost(4 * count * width, 4 * count * width * 2),
        name="embed_rows",
    )(ids, meta, table)


def mode_rows(first, step8, rows, store):
    run = list(first)
    for k in range(rows // SUB):
        total = run[0]
        for q in run[1:]:
            total = total + q
        store(k, total)
        if k + 1 < rows // SUB:
            run = [q * d for q, d in zip(run, step8)]


def spread(values, m):
    return jnp.broadcast_to(values[m : m + 1, :], (SUB, values.shape[1]))


def history_body(tiles, slot_total, meta, cache, rates_ref, resid_ref, states, taps):
    slots, rows, lanes = cache.shape
    step = pl.program_id(0)
    first_span, rank = meta[0], meta[1]
    rates = rates_ref[...]
    modes = rates.shape[0]
    decay = jnp.exp(-rates)

    def advance(i, held):
        base = pl.multiple_of(i * SUB, SUB)
        blocks = [cache[s, pl.ds(base, SUB), :] for s in range(slots)]
        for r in range(SUB):
            held = tuple(
                h * decay + jnp.broadcast_to(b[r : r + 1, :], (modes, lanes))
                for h, b in zip(held, blocks)
            )
        return held

    held = lax.fori_loop(
        0, rows // SUB, advance, tuple(jnp.zeros((modes, lanes), f32) for _ in range(slots))
    )
    part_a = jnp.zeros((modes, lanes), f32)
    part_b = jnp.zeros((modes, lanes), f32)
    for s in range(slots):
        slot = rank * slots + s
        age = lax.rem(first_span - slot - 1 + slot_total, slot_total) + 1
        far = (age * rows).astype(f32)
        kept = jnp.where(age < slot_total, 1.0, 0.0).astype(f32)
        part_a = part_a + (held[s] * decay) * jnp.exp(-rates * (far - float(rows)))
        part_b = part_b + (held[s] * decay) * (jnp.exp(-rates * far) * kept)
    states[0, 0] = part_a
    states[0, 1] = part_b

    @pl.when(step >= tiles)
    def _():
        place = lax.broadcasted_iota(jnp.int32, (SUB, lanes), 0).astype(f32)
        resid = resid_ref[...]
        step8 = jnp.exp(-rates * float(SUB))
        first = [
            spread(resid, m) * jnp.exp(-spread(rates, m) * place) for m in range(modes)
        ]

        def store(k, value):
            taps[k * SUB : (k + 1) * SUB, :] = value

        mode_rows(first, [spread(step8, m) for m in range(modes)], rows, store)


def history_states(meta, cache, rates, resid, half, slot_total):
    slots, rows, width = cache.shape
    modes = rates.shape[0]
    lanes = LANES
    tiles = half // lanes

    def lane_of(i, meta):
        rank = meta[1]
        return jnp.where(i < tiles, 1 - rank, rank) * tiles + lax.rem(i, tiles)

    return pl.pallas_call(
        functools.partial(history_body, tiles, slot_total),
        out_shape=(
            jax.ShapeDtypeStruct((2, 2, modes, half), f32),
            jax.ShapeDtypeStruct((rows, half), f32),
        ),
        grid_spec=pltpu.PrefetchScalarGridSpec(
            num_scalar_prefetch=1,
            grid=(2 * tiles,),
            in_specs=[
                pl.BlockSpec((slots, rows, lanes), lambda i, meta: (0, 0, lane_of(i, meta))),
                pl.BlockSpec((modes, lanes), lambda i, meta: (0, lane_of(i, meta))),
                pl.BlockSpec((modes, lanes), lambda i, meta: (0, lane_of(i, meta))),
            ],
            out_specs=(
                pl.BlockSpec(
                    (1, 2, modes, lanes), lambda i, meta: (i // tiles, 0, 0, lax.rem(i, tiles))
                ),
                pl.BlockSpec((rows, lanes), lambda i, meta: (0, jnp.maximum(i - tiles, 0))),
            ),
        ),
        compiler_params=params(),
        cost_estimate=cost(2 * slots * rows * modes * width, 4 * slots * rows * width),
        name="history_states",
    )(meta, cache, rates, resid)


def gate_body(
    channels, counts, meta, base, delta, gain, rates_ref, resid_ref, taps, *rest
):
    n_first, n_later, n_states = counts
    first_sums, rest = rest[:n_first], rest[n_first:]
    later_sums, rest = rest[:n_later], rest[n_later:]
    state_refs, rest = rest[:n_states], rest[n_states:]
    gated, end_state, scale, padded = rest
    rows, lanes = base.shape
    is_first = meta[2] == 1

    @pl.when(pl.program_id(0) == 0)
    def _():
        def total(refs):
            value = refs[0][0:1, :]
            for ref in refs[1:]:
                value = value + ref[0:1, :]
            return value

        sums = total(first_sums)
        if n_later:
            sums = jnp.where(is_first, sums, total(later_sums))
        wide = jnp.broadcast_to(sums, (rows, rows))
        here = lax.broadcasted_iota(jnp.int32, (rows, rows), 0)
        there = lax.broadcasted_iota(jnp.int32, (rows, rows), 1)
        column = jnp.sum(jnp.where(here == there, wide, 0.0), axis=1, keepdims=True)
        scale[...] = jnp.broadcast_to(
            lax.rsqrt(column / float(channels) + epsilon), scale.shape
        )
        padded[0:SUB, :] = jnp.zeros((SUB, lanes), f32)

    current = base[...]
    if delta is not None:
        current = current + jnp.where(is_first, 0.0, delta[...].astype(f32))
    normed = current * scale[...] * gain[...]
    padded[SUB:, :] = normed

    rates = rates_ref[...]
    modes = rates.shape[0]
    blocks = rows // SUB
    state = state_refs[0][...]
    for ref in state_refs[1:]:
        state = state + ref[...]
    weighted = resid_ref[...] * state
    step8 = jnp.exp(-rates * float(SUB))
    place = lax.broadcasted_iota(jnp.int32, (SUB, lanes), 0).astype(f32)
    first = [spread(weighted, m) * jnp.exp(-spread(rates, m) * place) for m in range(modes)]
    sums = [None] * blocks

    def store(k, value):
        sums[k] = value

    mode_rows(first, [spread(step8, m) for m in range(modes)], rows, store)
    for b in range(SUB):
        shifted = [
            padded[SUB + k * SUB - b : 2 * SUB + k * SUB - b, :] for k in range(blocks)
        ]
        for a in range(blocks):
            tap = jnp.broadcast_to(taps[a * SUB + b : a * SUB + b + 1, :], (SUB, lanes))
            for k in range(a, blocks):
                sums[k] = sums[k] + tap * shifted[k - a]
    for k in range(blocks):
        at = pl.ds(SUB + k * SUB, SUB)
        gated[k * SUB : (k + 1) * SUB, :] = (padded[at, :] * sums[k]).astype(gated.dtype)

    if end_state is not None:
        decay = jnp.exp(-rates)
        held = jnp.zeros((modes, lanes), f32)
        for r in range(rows):
            held = held * decay + jnp.broadcast_to(
                padded[SUB + r : SUB + r + 1, :], (modes, lanes)
            )
        end_state[...] = held * decay


def gate(meta, base, delta, gain, rates, resid, taps, first_sums, later_sums, states, channels, want_state, span):
    rows, half = base.shape[0] // 2, base.shape[1]
    modes = rates.shape[0]
    lanes = LANES
    tiles = half // lanes

    def lane_here(i, meta):
        return (0, meta[1] * tiles + i)

    in_specs = [pl.BlockSpec((rows, lanes), lambda i, meta: (span, i))]
    operands = [base]
    if delta is not None:
        in_specs.append(pl.BlockSpec((rows, lanes), lambda i, meta: (0, i)))
        operands.append(delta)
    in_specs += [
        pl.BlockSpec((1, lanes), lane_here),
        pl.BlockSpec((modes, lanes), lane_here),
        pl.BlockSpec((modes, lanes), lane_here),
        pl.BlockSpec((rows, lanes), lambda i, meta: (0, i)),
    ]
    operands += [gain, rates, resid, taps]
    for ref in first_sums:
        in_specs.append(pl.BlockSpec((pl.Squeezed(), SUB, rows), lambda i, meta: (span, 0, 0)))
        operands.append(ref)
    for ref in later_sums:
        in_specs.append(pl.BlockSpec((SUB, rows), lambda i, meta: (0, 0)))
        operands.append(ref)
    for ref in states:
        lead = ref.ndim - 2
        if lead == 0:
            in_specs.append(pl.BlockSpec((modes, lanes), lambda i, meta: (0, i)))
        elif lead == 1:
            in_specs.append(
                pl.BlockSpec((pl.Squeezed(), modes, lanes), lambda i, meta: (span, 0, i))
            )
        else:
            in_specs.append(
                pl.BlockSpec(
                    (pl.Squeezed(), pl.Squeezed(), modes, lanes), lambda i, meta: (1, span, 0, i)
                )
            )
        operands.append(ref)
    counts = (len(first_sums), len(later_sums), len(states))
    out_shape = [jax.ShapeDtypeStruct((rows, half), jnp.bfloat16)]
    out_specs = [pl.BlockSpec((rows, lanes), lambda i, meta: (0, i))]
    if want_state:
        out_shape.append(jax.ShapeDtypeStruct((modes, half), f32))
        out_specs.append(pl.BlockSpec((modes, lanes), lambda i, meta: (0, i)))

    def body(meta, *refs):
        refs = list(refs)
        base_ref = refs.pop(0)
        delta_ref = refs.pop(0) if delta is not None else None
        if not want_state:
            refs.insert(len(refs) - 2, None)
        gate_body(channels, counts, meta, base_ref, delta_ref, *refs)

    return pl.pallas_call(
        body,
        out_shape=tuple(out_shape),
        grid_spec=pltpu.PrefetchScalarGridSpec(
            num_scalar_prefetch=1,
            grid=(tiles,),
            in_specs=in_specs,
            out_specs=tuple(out_specs),
            scratch_shapes=[
                pltpu.VMEM((rows, lanes), f32),
                pltpu.VMEM((rows + SUB, lanes), f32),
            ],
        ),
        compiler_params=params(),
        cost_estimate=cost(rows * rows * half + 4 * modes * rows * half, 12 * rows * half),
        name="gate",
    )(meta, *operands)


def mix_body(flags, parts, blocks, *refs):
    has_acc, final, has_delta = flags
    refs = list(refs)
    pieces = [refs.pop(0) for _ in range(parts)]
    weight = refs.pop(0)
    acc_in = refs.pop(0) if has_acc else None
    base = refs.pop(0) if final else None
    delta = refs.pop(0) if final and has_delta else None
    if final:
        x_out, delta_out, sums_out, acc = refs
    else:
        (acc,) = refs
    part, step = pl.program_id(0), pl.program_id(1)
    depth = weight.shape[0]

    @pl.when(jnp.logical_and(part == 0, step == 0))
    def _():
        acc[...] = acc_in[...] if has_acc else jnp.zeros_like(acc)

    at = pl.ds(pl.multiple_of(step * depth, depth), depth)
    for p in range(parts):

        @pl.when(part == p)
        def _():
            acc[...] += jnp.dot(pieces[p][:, at], weight[...], preferred_element_type=f32)

    if final:

        @pl.when(jnp.logical_and(part == parts - 1, step == pl.num_programs(1) - 1))
        def _():
            moved = acc[...]
            if has_delta:
                moved = moved + jnp.where(blocks[parts] == 1, 0.0, delta[...].astype(f32))
            fresh = base[...] + moved
            x_out[...] = fresh
            delta_out[...] = moved.astype(delta_out.dtype)
            sums_out[...] = row_sums(lane_tiles_squared(fresh))


def mix(blocks, pieces, weight, acc, base, delta, final, span):
    rows, depth = pieces[0].shape
    out = weight.shape[1]
    parts = len(pieces)
    steps = max(1, depth // 512)
    tile = depth // steps
    whole = pl.BlockSpec((rows, out), lambda i, j, blocks: (0, 0))
    in_specs = [pl.BlockSpec((rows, depth), lambda i, j, blocks: (0, 0))] * parts
    in_specs.append(pl.BlockSpec((tile, out), lambda i, j, blocks: (blocks[i] * steps + j, 0)))
    operands = [*pieces, weight]
    if acc is not None:
        in_specs.append(whole)
        operands.append(acc)
    out_shape = jax.ShapeDtypeStruct((rows, out), f32)
    out_specs = whole
    scratch = []
    if final:
        in_specs.append(pl.BlockSpec((rows, out), lambda i, j, blocks: (span, 0)))
        operands.append(base)
        if delta is not None:
            in_specs.append(whole)
            operands.append(delta)
        out_shape = (
            out_shape,
            jax.ShapeDtypeStruct((rows, out), jnp.bfloat16),
            jax.ShapeDtypeStruct((SUB, rows), f32),
        )
        out_specs = (whole, whole, pl.BlockSpec((SUB, rows), lambda i, j, blocks: (0, 0)))
        scratch = [pltpu.VMEM((rows, out), f32)]
    return pl.pallas_call(
        functools.partial(mix_body, (acc is not None, final, delta is not None), parts),
        out_shape=out_shape,
        grid_spec=pltpu.PrefetchScalarGridSpec(
            num_scalar_prefetch=1,
            grid=(parts, steps),
            in_specs=in_specs,
            out_specs=out_specs,
            scratch_shapes=scratch,
        ),
        compiler_params=params(),
        cost_estimate=cost(2 * rows * depth * out * parts, 2 * depth * out * parts),
        name="mix",
    )(blocks, *operands)


def ring_order(count):
    return list(range(0, 1)) + list(range(1, count, 2)) + list(range(2, count, 2))[::-1]


def local(token_ids, leading_span_index, embed_table, norm_gain, decay_rates, residues, history, mix_weight):
    section_rank = lax.axis_index("section")
    sections = lax.axis_size("section")
    seq_rank = lax.axis_index("seq")
    seqs = lax.axis_size("seq")
    tensor_rank = lax.axis_index("tensor")
    tensors = lax.axis_size("tensor")
    rates, resid, cache, weight = decay_rates[0], residues[0], history[0], mix_weight[0]
    spans, rows = token_ids.shape
    slots, _, width = cache.shape
    half = weight.shape[1]
    channels = weight.shape[0]
    slot_total = slots * seqs
    order = ring_order(tensors)
    place = jnp.array([order.index(t) for t in range(tensors)], jnp.int32)[tensor_rank]
    order_array = jnp.array(order, jnp.int32)

    def along_ring(value, shift):
        return lax.ppermute(
            value, "tensor", [(order[i], order[(i + shift) % tensors]) for i in range(tensors)]
        )

    def swapped(value):
        return lax.ppermute(value, "seq", [(i, seqs - 1 - i) for i in range(seqs)])

    def to_next(value):
        return lax.ppermute(value, "section", [(i, (i + 1) % sections) for i in range(sections)])

    def to_next_shifted(value, shift):
        route = []
        for i in range(tensors):
            for s in range(sections):
                here = order[i] * sections + s
                there = order[(i + shift) % tensors] * sections + (s + 1) % sections
                route.append((here, there))
        return lax.ppermute(value, ("tensor", "section"), route)

    first_span = lax.rem(leading_span_index[0], slot_total)
    is_first = (section_rank == 0).astype(jnp.int32)
    meta = jnp.stack([first_span, seq_rank, is_first]).astype(jnp.int32)

    base, sums = embed_rows(token_ids.reshape(-1), meta, embed_table, half)
    sums = sums.reshape(SUB, spans, rows).transpose(1, 0, 2)
    small_ring = tensors <= 8
    if small_ring:
        first_sums = [sums] + [along_ring(sums, k) for k in range(1, tensors)]
    else:
        first_sums = [lax.psum(sums, "tensor")]
    states, taps = history_states(meta, cache, rates, resid, half, slot_total)
    partner = swapped(states[0])

    flag = is_first[None]
    blocks = []
    for k in range(tensors):
        source = order_array[lax.rem(place - k + tensors, tensors)]
        blocks.append(
            jnp.stack([source * seqs + seq_rank, source * seqs + seqs - 1 - seq_rank, is_first])
        )

    deltas = [None] * spans
    later_sums = [[]] * spans
    for stage in range(sections):
        gates = []
        held = []
        for span in range(spans):
            got = gate(
                meta, base, deltas[span], norm_gain, rates, resid, taps, first_sums, later_sums[span],
                [states, partner] + held, channels, span + 1 < spans, span,
            )
            gates.append(got[0])
            held = list(got[1:])
        results = []
        if small_ring:
            moving = list(gates)
            accs = [None] * spans
            for k in range(tensors):
                pairs = [[piece, swapped(piece)] for piece in moving]
                if k + 1 < tensors:
                    moving = [along_ring(piece, 1) for piece in moving]
                for span in range(spans):
                    last = k + 1 == tensors
                    accs[span] = mix(
                        blocks[k], pairs[span], weight, accs[span], base, deltas[span], last, span
                    )
            results = accs
        else:
            order_all = jnp.stack([jnp.int32(0), is_first])
            for span in range(spans):
                full = lax.all_gather(gates[span], ("tensor", "seq"), axis=1, tiled=True)
                results.append(
                    mix(order_all, [full], weight, None, base, deltas[span], True, span)
                )
        if stage + 1 < sections:
            new_deltas, new_sums = [], []
            for span in range(spans):
                _, moved, partial = results[span]
                new_deltas.append(to_next(moved))
                both = partial + swapped(partial)
                if small_ring:
                    new_sums.append([to_next_shifted(both, k) for k in range(tensors)])
                else:
                    new_sums.append([to_next(lax.psum(both, "tensor"))])
            deltas, later_sums = new_deltas, new_sums
    return jnp.stack([r[0] for r in results])[None]


def solution(mesh):
    placed = (
        P("groups", None),
        P("groups"),
        P(None, "tensor"),
        P("section", "tensor"),
        P("section", None, "tensor"),
        P("section", None, "tensor"),
        P("section", "seq", "groups", "tensor"),
        P("section", None, ("tensor", "seq")),
    )
    return jax.shard_map(
        local,
        mesh=mesh,
        in_specs=placed,
        out_specs=P("section", None, "groups", ("tensor", "seq")),
        check_vma=False,
    )
```

```python
import functools

import jax
import jax.numpy as jnp
from jax import lax
from jax.experimental import pallas as pl
from jax.experimental.pallas import tpu as pltpu
from jax.sharding import PartitionSpec as P


epsilon = 1e-05
highest = lax.Precision.HIGHEST
LANES = 128
SUB = 8
f32 = jnp.float32
VMEM_BYTES = 24 << 20


def params(**more):
    return pltpu.CompilerParams(vmem_limit_bytes=VMEM_BYTES, **more)


def in_hbm(value):
    return pltpu.with_memory_space_constraint(value, pltpu.HBM)


def cost(flops, moved):
    return pl.CostEstimate(flops=int(flops), bytes_accessed=int(moved), transcendentals=0)


def row_sums(squares):
    ones = jnp.ones((SUB, squares.shape[1]), f32)
    return lax.dot_general(
        ones, squares, (((1,), (1,)), ((), ())), precision=highest, preferred_element_type=f32
    )


def lane_tiles_squared(block):
    total = block[:, :LANES] * block[:, :LANES]
    for start in range(LANES, block.shape[1], LANES):
        piece = block[:, start : start + LANES]
        total = total + piece * piece
    return total


def embed_body(chunks, ids, meta, table, x_out, sums_out, held, rows_buf, sems):
    spans, rows = sums_out.shape[0], sums_out.shape[2]
    half = x_out.shape[2]
    width = held.shape[1]
    depth = held.shape[0] // chunks
    copies = [
        pltpu.make_async_copy(
            table.at[pl.ds(c * depth, depth), :], held.at[pl.ds(c * depth, depth), :], sems.at[c]
        )
        for c in range(chunks)
    ]
    for copy in copies:
        copy.start()
    for copy in copies:
        copy.wait()
    for span in range(spans):

        def fetch(i, carry):
            rows_buf[pl.ds(i, 1), :] = held[pl.ds(ids[span, i], 1), :]
            return carry

        lax.fori_loop(0, rows, fetch, 0, unroll=8)
        sums_out[span] = row_sums(lane_tiles_squared(rows_buf[...]))
        for part in range(width // half):

            @pl.when(meta[1] == part)
            def _():
                x_out[span] = rows_buf[:, part * half : (part + 1) * half]


def embed_rows(ids, meta, table, half):
    spans, rows = ids.shape
    words, width = table.shape
    chunks = 4 if words % (4 * SUB) == 0 else 1
    return pl.pallas_call(
        functools.partial(embed_body, chunks),
        out_shape=(
            jax.ShapeDtypeStruct((spans, rows, half), f32),
            jax.ShapeDtypeStruct((spans, SUB, rows), f32),
        ),
        in_specs=[
            pl.BlockSpec(memory_space=pltpu.SMEM),
            pl.BlockSpec(memory_space=pltpu.SMEM),
            pl.BlockSpec(memory_space=pl.ANY),
        ],
        out_specs=(
            pl.BlockSpec(memory_space=pltpu.VMEM),
            pl.BlockSpec(memory_space=pltpu.VMEM),
        ),
        scratch_shapes=[
            pltpu.VMEM((words, width), f32),
            pltpu.VMEM((rows, width), f32),
            pltpu.SemaphoreType.DMA((chunks,)),
        ],
        compiler_params=params(),
        cost_estimate=cost(4 * spans * rows * width, 4 * words * width),
        name="embed_rows",
    )(ids, meta, in_hbm(table))


def mode_rows(first, step8, rows, store):
    run = list(first)
    for k in range(rows // SUB):
        total = run[0]
        for q in run[1:]:
            total = total + q
        store(k, total)
        if k + 1 < rows // SUB:
            run = [q * d for q, d in zip(run, step8)]


def spread(values, m):
    return jnp.broadcast_to(values[m : m + 1, :], (SUB, values.shape[1]))


def history_body(chunk, wide, slot_total, meta, cache, rates_any, resid_any, *rest):
    states, taps, rates_out, resid_out, held_rows, rates_ref, resid_ref, sems, mode_sems = rest
    slots, rows, _ = cache.shape
    half = taps.shape[1]
    modes = rates_ref.shape[0]
    per_half = half // chunk
    first_span, rank = meta[0], meta[1]

    def lane_start(j):
        part = 1 - rank if j < per_half else rank
        return pl.multiple_of(part * half + (j % per_half) * chunk, LANES)

    copies = [
        pltpu.make_async_copy(
            cache.at[:, :, pl.ds(lane_start(j), chunk)],
            held_rows.at[:, :, pl.ds(j * chunk, chunk)],
            sems.at[j],
        )
        for j in range(2 * per_half)
    ]
    mode_copies = [
        pltpu.make_async_copy(rates_any, rates_ref, mode_sems.at[0]),
        pltpu.make_async_copy(resid_any, resid_ref, mode_sems.at[1]),
    ]
    for copy in mode_copies + copies:
        copy.start()
    for copy in mode_copies:
        copy.wait()
    own = pl.ds(pl.multiple_of(rank * half, LANES), half)
    rates_out[...] = rates_ref[:, own]
    resid_out[...] = resid_ref[:, own]

    for j in range(2 * per_half):
        copies[j].wait()

        def one_tile(t, carry, j=j):
            at = pl.ds(pl.multiple_of(j * chunk + t * wide, LANES), wide)
            rates = rates_ref[:, pl.ds(pl.multiple_of(lane_start(j) + t * wide, LANES), wide)]
            decay = jnp.exp(-rates)

            def advance(i, held):
                base = pl.multiple_of(i * SUB, SUB)
                block = [held_rows[s, pl.ds(base, SUB), at] for s in range(slots)]
                for r in range(SUB):
                    held = tuple(
                        h * decay + jnp.broadcast_to(block[s][r : r + 1, :], (modes, wide))
                        for s, h in enumerate(held)
                    )
                return held

            held = lax.fori_loop(
                0,
                rows // SUB,
                advance,
                tuple(jnp.zeros((modes, wide), f32) for _ in range(slots)),
            )
            part_a = jnp.zeros((modes, wide), f32)
            part_b = jnp.zeros((modes, wide), f32)
            for s in range(slots):
                slot = rank * slots + s
                age = lax.rem(first_span - slot - 1 + slot_total, slot_total) + 1
                far = (age * rows).astype(f32)
                kept = jnp.where(age < slot_total, 1.0, 0.0).astype(f32)
                part_a = part_a + (held[s] * decay) * jnp.exp(-rates * (far - float(rows)))
                part_b = part_b + (held[s] * decay) * (jnp.exp(-rates * far) * kept)
            out_at = pl.ds(pl.multiple_of((j % per_half) * chunk + t * wide, LANES), wide)
            states[j // per_half, 0, :, out_at] = part_a
            states[j // per_half, 1, :, out_at] = part_b
            return carry

        lax.fori_loop(0, chunk // wide, one_tile, 0)

    def tap_tile(t, carry):
        at = pl.ds(pl.multiple_of(rank * half + t * LANES, LANES), LANES)
        out_at = pl.ds(pl.multiple_of(t * LANES, LANES), LANES)
        rates, resid = rates_ref[:, at], resid_ref[:, at]
        place = lax.broadcasted_iota(jnp.int32, (SUB, LANES), 0).astype(f32)
        step8 = jnp.exp(-rates * float(SUB))
        first = [spread(resid, m) * jnp.exp(-spread(rates, m) * place) for m in range(modes)]

        def store(k, value):
            taps[k * SUB : (k + 1) * SUB, out_at] = value

        mode_rows(first, [spread(step8, m) for m in range(modes)], rows, store)
        return carry

    lax.fori_loop(0, half // LANES, tap_tile, 0)


def history_states(meta, cache, rates, resid, half, slot_total):
    slots, rows, width = cache.shape
    modes = rates.shape[0]
    chunk = 512 if half % 512 == 0 else LANES
    wide = 2 * LANES if chunk % (2 * LANES) == 0 else LANES
    vmem = pl.BlockSpec(memory_space=pltpu.VMEM)
    return pl.pallas_call(
        functools.partial(history_body, chunk, wide, slot_total),
        out_shape=(
            jax.ShapeDtypeStruct((2, 2, modes, half), f32),
            jax.ShapeDtypeStruct((rows, half), f32),
            jax.ShapeDtypeStruct((modes, half), f32),
            jax.ShapeDtypeStruct((modes, half), f32),
        ),
        in_specs=[pl.BlockSpec(memory_space=pltpu.SMEM)] + [pl.BlockSpec(memory_space=pl.ANY)] * 3,
        out_specs=(vmem, vmem, vmem, vmem),
        scratch_shapes=[
            pltpu.VMEM((slots, rows, width), f32),
            pltpu.VMEM((modes, width), f32),
            pltpu.VMEM((modes, width), f32),
            pltpu.SemaphoreType.DMA((2 * half // chunk,)),
            pltpu.SemaphoreType.DMA((2,)),
        ],
        compiler_params=params(),
        cost_estimate=cost(2 * slots * rows * modes * width, 4 * slots * rows * width),
        name="history_states",
    )(meta, in_hbm(cache), in_hbm(rates), in_hbm(resid))


def gate_body(channels, span, counts, meta, base, *rest):
    n_delta, n_first, n_later, n_before, n_out = counts
    rest = list(rest)

    def take(n):
        return [rest.pop(0) for _ in range(n)]

    delta = take(n_delta)
    gain, rates_ref, resid_ref, taps, mine, theirs = take(6)
    first_sums, later_sums, before = take(n_first), take(n_later), take(n_before)
    gated = rest.pop(0)
    normed_out = take(n_out)
    padded, state_buf = rest
    rows, half = gated.shape
    modes = rates_ref.shape[0]
    blocks = rows // SUB
    is_first = meta[2] == 1
    wide = 4 * LANES if half % (4 * LANES) == 0 else LANES

    if n_before:

        def chain(t, carry):
            at = pl.ds(pl.multiple_of(t * wide, LANES), wide)
            decay = jnp.exp(-rates_ref[:, at])

            def advance(i, held):
                block = before[0][pl.ds(pl.multiple_of(i * SUB, SUB), SUB), at]
                for r in range(SUB):
                    held = held * decay + jnp.broadcast_to(block[r : r + 1, :], (modes, wide))
                return held

            held = lax.fori_loop(0, blocks, advance, jnp.zeros((modes, wide), f32))
            state_buf[:, at] = held * decay + (mine[1, span, :, at] + theirs[span, :, at])
            return carry

        lax.fori_loop(0, half // wide, chain, 0)
    else:
        state_buf[...] = mine[1, span] + theirs[span]

    sums = first_sums[0][span, 0:1, :]
    for ref in first_sums[1:]:
        sums = sums + ref[span, 0:1, :]
    if n_later:
        later = later_sums[0][0:1, :]
        for ref in later_sums[1:]:
            later = later + ref[0:1, :]
        sums = jnp.where(is_first, sums, later)
    here = lax.broadcasted_iota(jnp.int32, (rows, rows), 0)
    there = lax.broadcasted_iota(jnp.int32, (rows, rows), 1)
    column = jnp.sum(
        jnp.where(here == there, jnp.broadcast_to(sums, (rows, rows)), 0.0), axis=1, keepdims=True
    )
    scale = jnp.broadcast_to(lax.rsqrt(column / float(channels) + epsilon), (rows, LANES))
    padded[0:SUB, :] = jnp.zeros((SUB, LANES), f32)

    def tile(t, carry):
        at = pl.ds(pl.multiple_of(t * LANES, LANES), LANES)
        own = pl.ds(pl.multiple_of(meta[1] * half + t * LANES, LANES), LANES)
        current = base[span, :, at]
        if n_delta:
            current = current + jnp.where(is_first, 0.0, delta[0][:, at].astype(f32))
        normed = current * scale * gain[:, own]
        padded[SUB:, :] = normed
        if n_out:
            normed_out[0][:, at] = normed
        rates = rates_ref[:, at]
        weighted = resid_ref[:, at] * state_buf[:, at]
        step8 = jnp.exp(-rates * float(SUB))
        place = lax.broadcasted_iota(jnp.int32, (SUB, LANES), 0).astype(f32)
        first = [spread(weighted, m) * jnp.exp(-spread(rates, m) * place) for m in range(modes)]
        total = [None] * blocks

        def store(k, value):
            total[k] = value

        mode_rows(first, [spread(step8, m) for m in range(modes)], rows, store)
        for b in range(SUB):
            shifted = [
                padded[SUB + k * SUB - b : 2 * SUB + k * SUB - b, :] for k in range(blocks)
            ]
            for a in range(blocks):
                j = a * SUB + b
                tap = jnp.broadcast_to(taps[j : j + 1, at], (SUB, LANES))
                for k in range(a, blocks):
                    total[k] = total[k] + tap * shifted[k - a]
        for k in range(blocks):
            rows_at = pl.ds(SUB + k * SUB, SUB)
            gated[k * SUB : (k + 1) * SUB, at] = (padded[rows_at, :] * total[k]).astype(gated.dtype)
        return carry

    lax.fori_loop(0, half // LANES, tile, 0)


def gate(meta, base, delta, gain, modes_here, taps, first_sums, later_sums, states, before, channels, span):
    spans, rows, half = base.shape
    modes = modes_here[0].shape[0]
    vmem = pl.BlockSpec(memory_space=pltpu.VMEM)
    deltas = [] if delta is None else [delta]
    want = int(span + 1 < spans)
    operands = [base, *deltas, gain, *modes_here, taps, *states, *first_sums, *later_sums, *before]
    counts = (len(deltas), len(first_sums), len(later_sums), len(before), want)
    out_shape = [jax.ShapeDtypeStruct((rows, half), jnp.bfloat16)]
    if want:
        out_shape.append(jax.ShapeDtypeStruct((rows, half), f32))
    return pl.pallas_call(
        functools.partial(gate_body, channels, span, counts),
        out_shape=tuple(out_shape),
        in_specs=[pl.BlockSpec(memory_space=pltpu.SMEM)] + [vmem] * len(operands),
        out_specs=tuple(vmem for _ in out_shape),
        scratch_shapes=[pltpu.VMEM((rows + SUB, LANES), f32), pltpu.VMEM((modes, half), f32)],
        compiler_params=params(),
        cost_estimate=cost(rows * rows * half + 4 * modes * rows * half, 12 * rows * half),
        name="gate",
    )(meta, *operands)


def mix_body(kind, chosen, counts, out_tile, blocks, *refs):
    parts, n_acc, n_base, n_delta, n_done = counts
    refs = list(refs)

    def take(n):
        return [refs.pop(0) for _ in range(n)]

    pieces = [take(len(chosen)) for _ in range(parts)]
    (weight,) = take(1)
    acc_in, base, delta, done = take(n_acc), take(n_base), take(n_delta), take(n_done)
    held, sems = refs[-2:]
    rows, depth = pieces[0][0].shape
    out = weight.shape[1]
    tiles = out // out_tile
    copies = []
    for n in range(tiles):
        for p in range(parts):
            at = pl.ds(pl.multiple_of(blocks[p] * depth, depth), depth)
            columns = pl.ds(n * out_tile, out_tile)
            copies.append(
                pltpu.make_async_copy(
                    weight.at[at, columns], held.at[p, :, columns], sems.at[n * parts + p]
                )
            )
    for copy in copies:
        copy.start()
    span = chosen[0]
    squares = jnp.zeros((rows, LANES), f32)
    for n in range(tiles):
        at = slice(n * out_tile, (n + 1) * out_tile)
        for p in range(parts):
            copies[n * parts + p].wait()
        total = None
        for p in range(parts):
            lhs = jnp.concatenate([piece[...] for piece in pieces[p]], axis=0)
            more = jnp.dot(lhs, held[p, :, at], preferred_element_type=f32)
            total = more if total is None else total + more
        if n_acc and acc_in[0].shape[0] == total.shape[0]:
            total = total + acc_in[0][:, at]
        elif n_acc:
            total = total + acc_in[0][span * rows : (span + 1) * rows, at]
        if kind == "part":
            refs[0][:, at] = total
            continue
        if n_delta:
            total = total + jnp.where(blocks[parts] == 1, 0.0, delta[0][:, at].astype(f32))
        fresh = base[0][span, :, at] + total
        if kind == "hop":
            refs[0][:, at] = total.astype(refs[0].dtype)
            squares = squares + lane_tiles_squared(fresh)
        elif kind == "done":
            refs[0][:, at] = fresh
        else:
            refs[0][0, span, :, at] = fresh
            for i, ref in enumerate(done):
                refs[0][0, i, :, at] = ref[:, at]
    if kind == "hop":
        refs[1][...] = row_sums(squares)


def mix(kind, blocks, pieces, chosen, weight, acc, base, delta, done=()):
    rows, depth = pieces[0][0].shape
    out = weight.shape[1]
    vmem = pl.BlockSpec(memory_space=pltpu.VMEM)
    accs = [] if acc is None else [acc]
    bases = [] if kind == "part" else [base]
    deltas = [] if kind == "part" or delta is None else [delta]
    flat = [piece for part in pieces for piece in part]
    operands = [*flat, in_hbm(weight), *accs, *bases, *deltas, *done]
    counts = (len(pieces), len(accs), len(bases), len(deltas), len(done))
    whole = jax.ShapeDtypeStruct((rows * len(chosen), out), f32)
    out_shape, out_specs = whole, vmem
    if kind == "hop":
        out_shape = (
            jax.ShapeDtypeStruct((rows, out), jnp.bfloat16),
            jax.ShapeDtypeStruct((SUB, rows), f32),
        )
        out_specs = (vmem, vmem)
    elif kind == "out":
        out_shape = jax.ShapeDtypeStruct((1, len(done) + 1, rows, out), f32)
    out_tile = 4 * LANES if out % (4 * LANES) == 0 else LANES
    in_specs = [vmem] * len(operands)
    in_specs[len(flat)] = pl.BlockSpec(memory_space=pl.ANY)
    return pl.pallas_call(
        functools.partial(mix_body, kind, chosen, counts, out_tile),
        out_shape=out_shape,
        in_specs=[pl.BlockSpec(memory_space=pltpu.SMEM)] + in_specs,
        out_specs=out_specs,
        scratch_shapes=[
            pltpu.VMEM((len(pieces), depth, out), weight.dtype),
            pltpu.SemaphoreType.DMA((len(pieces) * (out // out_tile),)),
        ],
        compiler_params=params(),
        cost_estimate=cost(
            2 * rows * len(chosen) * depth * out * len(pieces), 2 * depth * out * len(pieces)
        ),
    )(blocks, *operands)


def ring_order(count):
    return list(range(0, 1)) + list(range(1, count, 2)) + list(range(2, count, 2))[::-1]


def local(token_ids, leading_span_index, embed_table, norm_gain, decay_rates, residues, history, mix_weight):
    section_rank = lax.axis_index("section")
    sections = lax.axis_size("section")
    seq_rank = lax.axis_index("seq")
    seqs = lax.axis_size("seq")
    tensor_rank = lax.axis_index("tensor")
    tensors = lax.axis_size("tensor")
    rates, resid, cache, weight = decay_rates[0], residues[0], history[0], mix_weight[0]
    spans, _ = token_ids.shape
    slots, _, _ = cache.shape
    half = weight.shape[1]
    channels = weight.shape[0]
    slot_total = slots * seqs
    order = ring_order(tensors)
    place = jnp.array([order.index(t) for t in range(tensors)], jnp.int32)[tensor_rank]
    order_array = jnp.array(order, jnp.int32)

    def along_ring(value, shift):
        return lax.ppermute(
            value, "tensor", [(order[i], order[(i + shift) % tensors]) for i in range(tensors)]
        )

    def swapped(value):
        return lax.ppermute(value, "seq", [(i, seqs - 1 - i) for i in range(seqs)])

    def to_next(value):
        return lax.ppermute(value, "section", [(i, (i + 1) % sections) for i in range(sections)])

    def to_next_shifted(value, shift):
        route = []
        for i in range(tensors):
            for s in range(sections):
                here = order[i] * sections + s
                there = order[(i + shift) % tensors] * sections + (s + 1) % sections
                route.append((here, there))
        return lax.ppermute(value, ("tensor", "section"), route)

    first_span = lax.rem(leading_span_index[0], slot_total)
    is_first = (section_rank == 0).astype(jnp.int32)
    meta = jnp.stack([first_span, seq_rank, is_first]).astype(jnp.int32)

    base, sums = embed_rows(token_ids, meta, embed_table, half)
    small_ring = tensors <= 8
    first_sums = [sums]
    if small_ring:
        for k in range(1, tensors):
            first_sums.append(along_ring(sums, k))
    else:
        first_sums = [lax.psum(sums, "tensor")]
    states, taps, *modes_here = history_states(meta, cache, rates, resid, half, slot_total)
    partner = swapped(states[0])

    blocks = []
    for k in range(tensors):
        source = order_array[lax.rem(place - k + tensors, tensors)]
        blocks.append(
            jnp.stack([source * seqs + seq_rank, source * seqs + seqs - 1 - seq_rank, is_first])
        )

    every = tuple(range(spans))
    deltas = [None] * spans
    later_sums = [[]] * spans
    order_all = jnp.stack([jnp.int32(0), is_first])
    for stage in range(sections):
        last_stage = stage + 1 == sections
        gates = []
        before = []
        for span in every:
            got = gate(
                meta, base, deltas[span], norm_gain, modes_here, taps, first_sums,
                later_sums[span], [states, partner], before, channels, span,
            )
            gates.append(got[0])
            before = list(got[1:])
        acc = None
        moving = list(gates)
        results = []
        steps = tensors if small_ring else 1
        for k in range(steps):
            final = k + 1 == steps
            if small_ring:
                rows_of = blocks[k]
                crossed = []
                for span in every:
                    crossed.append(swapped(moving[span]))
                pairs = [list(moving), crossed]
                if not final:
                    for span in every:
                        moving[span] = along_ring(moving[span], 1)
            else:
                rows_of = order_all
                pairs = [[lax.all_gather(g, ("tensor", "seq"), axis=1, tiled=True) for g in gates]]
            if not final:
                acc = mix("part", rows_of, pairs, every, weight, acc, None, None)
                continue
            for span in every:
                kind = "hop" if not last_stage else "out" if span + 1 == spans else "done"
                done = tuple(results) if kind == "out" else ()
                results.append(
                    mix(
                        kind, rows_of, [[part[span]] for part in pairs], (span,), weight, acc,
                        base, deltas[span], done,
                    )
                )
        if not last_stage:
            new_deltas, new_sums = [], []
            for span in every:
                moved, partial = results[span]
                new_deltas.append(to_next(moved))
                both = partial + swapped(partial)
                if small_ring:
                    got = []
                    for k in range(tensors):
                        got.append(to_next_shifted(both, k))
                    new_sums.append(got)
                else:
                    new_sums.append([to_next(lax.psum(both, "tensor"))])
            deltas, later_sums = new_deltas, new_sums
    return results[-1]


def solution(mesh):
    placed = (
        P("groups", None),
        P("groups"),
        P(None, "tensor"),
        P("section", "tensor"),
        P("section", None, "tensor"),
        P("section", None, "tensor"),
        P("section", "seq", "groups", "tensor"),
        P("section", None, ("tensor", "seq")),
    )
    return jax.shard_map(
        local,
        mesh=mesh,
        in_specs=placed,
        out_specs=P("section", None, "groups", ("tensor", "seq")),
        check_vma=False,
    )
```

```python
import functools

import jax
import jax.numpy as jnp
from jax import lax
from jax.experimental import pallas as pl
from jax.experimental.pallas import tpu as pltpu
from jax.sharding import PartitionSpec as P


epsilon = 1e-05
highest = lax.Precision.HIGHEST
LANES = 128
SUB = 8
f32 = jnp.float32
MIB = 1 << 20


def params(mib):
    return pltpu.CompilerParams(vmem_limit_bytes=mib * MIB)


def in_vmem(value):
    return pltpu.with_memory_space_constraint(value, pltpu.VMEM)


def row_spread(ref, row, at, lead=()):
    return ref.at[(*lead, slice(None), at)][pl.ds(row, SUB, stride=0), :]


def in_hbm(value):
    return pltpu.with_memory_space_constraint(value, pltpu.HBM)


def cost(flops, moved):
    return pl.CostEstimate(flops=int(flops), bytes_accessed=int(moved), transcendentals=0)


def row_sums(squares):
    ones = jnp.ones((SUB, squares.shape[1]), f32)
    return lax.dot_general(
        ones, squares, (((1,), (1,)), ((), ())), precision=highest, preferred_element_type=f32
    )


def lane_tiles_squared(block):
    total = block[:, :LANES] * block[:, :LANES]
    for start in range(LANES, block.shape[1], LANES):
        piece = block[:, start : start + LANES]
        total = total + piece * piece
    return total


def embed_body(chunks, meta, ids_any, table, x_out, sums_out, ids, held, rows_buf, sems):
    spans, rows = sums_out.shape[0], sums_out.shape[2]
    half = x_out.shape[2]
    width = held.shape[1]
    depth = held.shape[0] // chunks
    copies = [
        pltpu.make_async_copy(
            table.at[pl.ds(c * depth, depth), :], held.at[pl.ds(c * depth, depth), :], sems.at[c]
        )
        for c in range(chunks)
    ]
    copies.append(pltpu.make_async_copy(ids_any, ids, sems.at[chunks]))
    for copy in copies:
        copy.start()
    for copy in copies:
        copy.wait()
    for span in range(spans):

        def fetch(i, carry):
            rows_buf[pl.ds(i, 1), :] = held[pl.ds(ids[span, i], 1), :]
            return carry

        lax.fori_loop(0, rows, fetch, 0, unroll=8)
        sums_out[span] = row_sums(lane_tiles_squared(rows_buf[...]))
        for part in range(width // half):

            @pl.when(meta[1] == part)
            def _():
                x_out[span] = rows_buf[:, part * half : (part + 1) * half]


def embed_rows(ids, meta, table, half):
    spans, rows = ids.shape
    words, width = table.shape
    chunks = 4 if words % (4 * SUB) == 0 else 1
    return pl.pallas_call(
        functools.partial(embed_body, chunks),
        out_shape=(
            jax.ShapeDtypeStruct((spans, rows, half), f32),
            jax.ShapeDtypeStruct((spans, SUB, rows), f32),
        ),
        in_specs=[
            pl.BlockSpec(memory_space=pltpu.SMEM),
            pl.BlockSpec(memory_space=pl.ANY),
            pl.BlockSpec(memory_space=pl.ANY),
        ],
        out_specs=(
            pl.BlockSpec(memory_space=pltpu.VMEM),
            pl.BlockSpec(memory_space=pltpu.VMEM),
        ),
        scratch_shapes=[
            pltpu.SMEM((spans, rows), jnp.int32),
            pltpu.VMEM((words, width), f32),
            pltpu.VMEM((rows, width), f32),
            pltpu.SemaphoreType.DMA((chunks + 1,)),
        ],
        compiler_params=params(8),
        cost_estimate=cost(4 * spans * rows * width, 4 * words * width),
        name="embed_rows",
    )(meta, in_hbm(ids), in_hbm(table))


def mode_rows(first, step8, rows, store):
    run = list(first)
    for k in range(rows // SUB):
        total = run[0]
        for q in run[1:]:
            total = total + q
        store(k, total)
        if k + 1 < rows // SUB:
            run = [q * d for q, d in zip(run, step8)]


def spread(values, m):
    return jnp.broadcast_to(values[m : m + 1, :], (SUB, values.shape[1]))


def history_body(chunk, wide, slot_total, meta, cache, rates_any, resid_any, weight, *rest):
    states, taps, rates_out, resid_out, weight_out = rest[:5]
    held_rows, rates_ref, resid_ref, sems, mode_sems = rest[5:]
    slots, rows, width = cache.shape
    half = taps.shape[1]
    modes = rates_ref.shape[0]
    chunks = width // chunk
    per_chunk = chunk // wide
    first_span, rank = meta[0], meta[1]

    def lane_start(tile):
        part = jnp.where(tile * wide < half, 1 - rank, rank)
        return pl.multiple_of(part * half + lax.rem(tile * wide, half), LANES)

    def fetch(j):
        return pltpu.make_async_copy(
            cache.at[:, :, pl.ds(lane_start(j * per_chunk), chunk)],
            held_rows.at[:, :, pl.ds(pl.multiple_of(j * chunk, LANES), chunk)],
            sems.at[j],
        )

    mode_copies = [
        pltpu.make_async_copy(rates_any, rates_ref, mode_sems.at[0]),
        pltpu.make_async_copy(resid_any, resid_ref, mode_sems.at[1]),
    ]
    weight_copy = pltpu.make_async_copy(weight, weight_out, mode_sems.at[2])
    for copy in mode_copies:
        copy.start()
    for j in range(chunks):
        fetch(j).start()
    weight_copy.start()
    for copy in mode_copies:
        copy.wait()
    own = pl.ds(pl.multiple_of(rank * half, LANES), half)
    rates_out[...] = rates_ref[:, own]
    resid_out[...] = resid_ref[:, own]

    def one_tile(t, carry):
        @pl.when(lax.rem(t, per_chunk) == 0)
        def _():
            fetch(t // per_chunk).wait()

        at = pl.ds(pl.multiple_of(t * wide, LANES), wide)
        rates = rates_ref[:, pl.ds(lane_start(t), wide)]
        decay = jnp.exp(-rates)
        groups = [decay[g : g + SUB, :] for g in range(0, modes, SUB)]
        held = [[jnp.zeros((SUB, wide), f32) for _ in groups] for _ in range(slots)]
        for r in range(rows):
            for s in range(slots):
                row = row_spread(held_rows, r, at, (s,))
                held[s] = [h * d + row for h, d in zip(held[s], groups)]
        part_a = jnp.zeros((modes, wide), f32)
        part_b = jnp.zeros((modes, wide), f32)
        for s in range(slots):
            slot = rank * slots + s
            age = lax.rem(first_span - slot - 1 + slot_total, slot_total) + 1
            far = (age * rows).astype(f32)
            kept = jnp.where(age < slot_total, 1.0, 0.0).astype(f32)
            total = jnp.concatenate(held[s], axis=0) * decay
            part_a = part_a + total * jnp.exp(-rates * (far - float(rows)))
            part_b = part_b + total * (jnp.exp(-rates * far) * kept)
        out_at = pl.ds(pl.multiple_of(lax.rem(t * wide, half), LANES), wide)
        side = (t * wide) // half
        states[side, 0, :, out_at] = part_a
        states[side, 1, :, out_at] = part_b
        return carry

    lax.fori_loop(0, width // wide, one_tile, 0)

    def tap_tile(t, carry):
        at = pl.ds(pl.multiple_of(rank * half + t * LANES, LANES), LANES)
        out_at = pl.ds(pl.multiple_of(t * LANES, LANES), LANES)
        rates, resid = rates_ref[:, at], resid_ref[:, at]
        place = lax.broadcasted_iota(jnp.int32, (SUB, LANES), 0).astype(f32)
        step8 = jnp.exp(-rates * float(SUB))
        first = [spread(resid, m) * jnp.exp(-spread(rates, m) * place) for m in range(modes)]

        def store(k, value):
            taps[k * SUB : (k + 1) * SUB, out_at] = value

        mode_rows(first, [spread(step8, m) for m in range(modes)], rows, store)
        return carry

    lax.fori_loop(0, half // LANES, tap_tile, 0)
    weight_copy.wait()


def history_states(meta, cache, rates, resid, weight, slot_total):
    slots, rows, width = cache.shape
    modes = rates.shape[0]
    half = weight.shape[1]
    chunk = 512 if half % 512 == 0 else LANES
    wide = 2 * LANES if chunk % (2 * LANES) == 0 else LANES
    vmem = pl.BlockSpec(memory_space=pltpu.VMEM)
    return pl.pallas_call(
        functools.partial(history_body, chunk, wide, slot_total),
        out_shape=(
            jax.ShapeDtypeStruct((2, 2, modes, half), f32),
            jax.ShapeDtypeStruct((rows, half), f32),
            jax.ShapeDtypeStruct((modes, half), f32),
            jax.ShapeDtypeStruct((modes, half), f32),
            pltpu.VMEM(weight.shape, weight.dtype),
        ),
        in_specs=[pl.BlockSpec(memory_space=pltpu.SMEM)] + [pl.BlockSpec(memory_space=pl.ANY)] * 4,
        out_specs=(vmem, vmem, vmem, vmem, vmem),
        scratch_shapes=[
            pltpu.VMEM((slots, rows, width), f32),
            pltpu.VMEM((modes, width), f32),
            pltpu.VMEM((modes, width), f32),
            pltpu.SemaphoreType.DMA((width // chunk,)),
            pltpu.SemaphoreType.DMA((3,)),
        ],
        compiler_params=params(6),
        cost_estimate=cost(2 * slots * rows * modes * width, 4 * slots * rows * width),
        name="history_states",
    )(meta, in_hbm(cache), in_hbm(rates), in_hbm(resid), in_hbm(weight))


def gate_body(channels, span, counts, meta, base, *rest):
    n_delta, n_first, n_later, n_before, n_out = counts
    rest = list(rest)

    def take(n):
        return [rest.pop(0) for _ in range(n)]

    delta = take(n_delta)
    gain, rates_ref, resid_ref, taps, mine, theirs = take(6)
    take(1)
    first_sums, later_sums, before = take(n_first), take(n_later), take(n_before)
    gated = rest.pop(0)
    normed_out = take(n_out)
    padded, state_buf = rest
    rows, half = gated.shape
    modes = rates_ref.shape[0]
    blocks = rows // SUB
    is_first = meta[2] == 1
    wide = 4 * LANES if half % (4 * LANES) == 0 else LANES

    if n_before:

        def chain(t, carry):
            at = pl.ds(pl.multiple_of(t * wide, LANES), wide)
            decay = jnp.exp(-rates_ref[:, at])
            groups = [decay[g : g + SUB, :] for g in range(0, modes, SUB)]
            held = [jnp.zeros((SUB, wide), f32) for _ in groups]
            for r in range(rows):
                row = row_spread(before[0], r, at)
                held = [h * d + row for h, d in zip(held, groups)]
            state_buf[:, at] = jnp.concatenate(held, axis=0) * decay + (
                mine[1, span, :, at] + theirs[span, :, at]
            )
            return carry

        lax.fori_loop(0, half // wide, chain, 0)
    else:
        state_buf[...] = mine[1, span] + theirs[span]

    sums = first_sums[0][span, 0:1, :]
    for ref in first_sums[1:]:
        sums = sums + ref[span, 0:1, :]
    if n_later:
        later = later_sums[0][0:1, :]
        for ref in later_sums[1:]:
            later = later + ref[0:1, :]
        sums = jnp.where(is_first, sums, later)
    here = lax.broadcasted_iota(jnp.int32, (rows, rows), 0)
    there = lax.broadcasted_iota(jnp.int32, (rows, rows), 1)
    column = jnp.sum(
        jnp.where(here == there, jnp.broadcast_to(sums, (rows, rows)), 0.0), axis=1, keepdims=True
    )
    scale = jnp.broadcast_to(lax.rsqrt(column / float(channels) + epsilon), (rows, LANES))
    padded[0:SUB, :] = jnp.zeros((SUB, LANES), f32)

    def tile(t, carry):
        at = pl.ds(pl.multiple_of(t * LANES, LANES), LANES)
        own = pl.ds(pl.multiple_of(meta[1] * half + t * LANES, LANES), LANES)
        current = base[span, :, at]
        if n_delta:
            current = current + jnp.where(is_first, 0.0, delta[0][:, at].astype(f32))
        normed = current * scale * gain[:, own]
        padded[SUB:, :] = normed
        if n_out:
            normed_out[0][:, at] = normed
        rates = rates_ref[:, at]
        weighted = resid_ref[:, at] * state_buf[:, at]
        step8 = jnp.exp(-rates * float(SUB))
        place = lax.broadcasted_iota(jnp.int32, (SUB, LANES), 0).astype(f32)
        first = [spread(weighted, m) * jnp.exp(-spread(rates, m) * place) for m in range(modes)]
        total = [None] * blocks

        def store(k, value):
            total[k] = value

        mode_rows(first, [spread(step8, m) for m in range(modes)], rows, store)
        for b in range(SUB):
            shifted = [
                padded[SUB + k * SUB - b : 2 * SUB + k * SUB - b, :] for k in range(blocks)
            ]
            for a in range(blocks):
                j = a * SUB + b
                tap = row_spread(taps, j, at)
                for k in range(a, blocks):
                    total[k] = total[k] + tap * shifted[k - a]
        for k in range(blocks):
            rows_at = pl.ds(SUB + k * SUB, SUB)
            gated[k * SUB : (k + 1) * SUB, at] = (padded[rows_at, :] * total[k]).astype(gated.dtype)
        return carry

    lax.fori_loop(0, half // LANES, tile, 0)


def gate(meta, base, delta, gain, modes_here, taps, weight, first_sums, later_sums, states, before, span):
    spans, rows, half = base.shape
    modes = modes_here[0].shape[0]
    vmem = pl.BlockSpec(memory_space=pltpu.VMEM)
    deltas = [] if delta is None else [delta]
    want = int(span + 1 < spans)
    head = [base, *deltas, gain, *modes_here, taps, *states]
    operands = [*head, in_vmem(weight), *first_sums, *later_sums, *before]
    in_specs = [vmem] * len(operands)
    in_specs[len(head)] = pl.BlockSpec(memory_space=pl.ANY)
    counts = (len(deltas), len(first_sums), len(later_sums), len(before), want)
    out_shape = [jax.ShapeDtypeStruct((rows, half), jnp.bfloat16)]
    if want:
        out_shape.append(jax.ShapeDtypeStruct((rows, half), f32))
    return pl.pallas_call(
        functools.partial(gate_body, weight.shape[0], span, counts),
        out_shape=tuple(out_shape),
        in_specs=[pl.BlockSpec(memory_space=pltpu.SMEM)] + in_specs,
        out_specs=tuple(vmem for _ in out_shape),
        scratch_shapes=[pltpu.VMEM((rows + SUB, LANES), f32), pltpu.VMEM((modes, half), f32)],
        compiler_params=params(2),
        cost_estimate=cost(rows * rows * half + 4 * modes * rows * half, 12 * rows * half),
        name="gate",
    )(meta, *operands)


def source_of(step, rank, count):
    place = jnp.where(lax.rem(rank, 2) == 1, (rank + 1) // 2, lax.rem(count - rank // 2, count))
    came = lax.rem(place - step + count, count)
    return jnp.where(came <= count // 2, jnp.maximum(2 * came - 1, 0), 2 * (count - came))


def mix_body(kind, chosen, counts, out_tile, step, meta, *refs):
    parts, n_acc, n_base, n_delta, n_done, seqs, tensors = counts
    refs = list(refs)

    def take(n):
        return [refs.pop(0) for _ in range(n)]

    pieces = [take(len(chosen)) for _ in range(parts)]
    (weight,) = take(1)
    acc_in, base, delta, done = take(n_acc), take(n_base), take(n_delta), take(n_done)
    rows, depth = pieces[0][0].shape
    out = weight.shape[1]
    if step is None:
        starts = [0] * parts
    else:
        source = source_of(step, meta[3], tensors) * seqs
        starts = [
            pl.multiple_of((source + jnp.where(p == 0, meta[1], seqs - 1 - meta[1])) * depth, depth)
            for p in range(parts)
        ]
    span = chosen[0]
    squares = jnp.zeros((rows, LANES), f32)
    for n in range(out // out_tile):
        at = slice(n * out_tile, (n + 1) * out_tile)
        total = None
        for p in range(parts):
            lhs = jnp.concatenate([piece[...] for piece in pieces[p]], axis=0)
            more = jnp.dot(lhs, weight[pl.ds(starts[p], depth), at], preferred_element_type=f32)
            total = more if total is None else total + more
        if n_acc and acc_in[0].shape[0] == total.shape[0]:
            total = total + acc_in[0][:, at]
        elif n_acc:
            total = total + acc_in[0][span * rows : (span + 1) * rows, at]
        if kind == "part":
            refs[0][:, at] = total
            continue
        if n_delta:
            total = total + jnp.where(meta[2] == 1, 0.0, delta[0][:, at].astype(f32))
        fresh = base[0][span, :, at] + total
        if kind == "hop":
            refs[0][:, at] = total.astype(refs[0].dtype)
            squares = squares + lane_tiles_squared(fresh)
        elif kind == "done":
            refs[0][:, at] = fresh
        else:
            refs[0][0, span, :, at] = fresh
            for i, ref in enumerate(done):
                refs[0][0, i, :, at] = ref[:, at]
    if kind == "hop":
        refs[1][...] = row_sums(squares)


def mix(kind, meta, step, pieces, chosen, weight, acc, base, delta, seqs, tensors, done=()):
    rows, depth = pieces[0][0].shape
    out = weight.shape[1]
    vmem = pl.BlockSpec(memory_space=pltpu.VMEM)
    accs = [] if acc is None else [acc]
    bases = [] if kind == "part" else [base]
    deltas = [] if kind == "part" or delta is None else [delta]
    flat = [piece for part in pieces for piece in part]
    operands = [*flat, in_vmem(weight), *accs, *bases, *deltas, *done]
    counts = (len(pieces), len(accs), len(bases), len(deltas), len(done), seqs, tensors)
    whole = jax.ShapeDtypeStruct((rows * len(chosen), out), f32)
    out_shape, out_specs = whole, vmem
    if kind == "hop":
        out_shape = (
            jax.ShapeDtypeStruct((rows, out), jnp.bfloat16),
            jax.ShapeDtypeStruct((SUB, rows), f32),
        )
        out_specs = (vmem, vmem)
    elif kind == "out":
        out_shape = jax.ShapeDtypeStruct((1, len(done) + 1, rows, out), f32)
    out_tile = 4 * LANES if out % (4 * LANES) == 0 else LANES
    return pl.pallas_call(
        functools.partial(mix_body, kind, chosen, counts, out_tile, step),
        out_shape=out_shape,
        in_specs=[pl.BlockSpec(memory_space=pltpu.SMEM)] + [vmem] * len(operands),
        out_specs=out_specs,
        compiler_params=params(8),
        cost_estimate=cost(
            2 * rows * len(chosen) * depth * out * len(pieces), 2 * depth * out * len(pieces)
        ),
    )(meta, *operands)


def ring_fits(tensors):
    return tensors in (2, 4, 8)


def ring_order(count):
    return list(range(0, 1)) + list(range(1, count, 2)) + list(range(2, count, 2))[::-1]


def local(token_ids, leading_span_index, embed_table, norm_gain, decay_rates, residues, history, mix_weight):
    section_rank = lax.axis_index("section")
    sections = lax.axis_size("section")
    seq_rank = lax.axis_index("seq")
    seqs = lax.axis_size("seq")
    tensor_rank = lax.axis_index("tensor")
    tensors = lax.axis_size("tensor")
    rates, resid, cache, weight = decay_rates[0], residues[0], history[0], mix_weight[0]
    spans, _ = token_ids.shape
    slots, _, _ = cache.shape
    half = weight.shape[1]
    slot_total = slots * seqs
    order = ring_order(tensors)

    def along_ring(value, shift):
        return lax.ppermute(
            value, "tensor", [(order[i], order[(i + shift) % tensors]) for i in range(tensors)]
        )

    def swapped(value):
        return lax.ppermute(value, "seq", [(i, seqs - 1 - i) for i in range(seqs)])

    def to_next(value):
        return lax.ppermute(value, "section", [(i, (i + 1) % sections) for i in range(sections)])

    def across(value, flip):
        return lax.ppermute(value, "tensor", [(i, i ^ flip) for i in range(tensors)])

    def to_next_across(value, flip):
        route = []
        for i in range(tensors):
            for s in range(sections):
                route.append((i * sections + s, (i ^ flip) * sections + (s + 1) % sections))
        return lax.ppermute(value, ("tensor", "section"), route)

    first_span = lax.rem(leading_span_index[0], slot_total)
    is_first = (section_rank == 0).astype(jnp.int32)
    meta = jnp.stack([first_span, seq_rank, is_first, tensor_rank]).astype(jnp.int32)

    base, sums = embed_rows(token_ids, meta, embed_table, half)
    small_ring = ring_fits(tensors)
    first_sums = [sums]
    if small_ring:
        for k in range(1, tensors):
            first_sums.append(along_ring(sums, k))
    else:
        first_sums = [lax.psum(sums, "tensor")]
    states, taps, *modes_here = history_states(meta, cache, rates, resid, weight, slot_total)
    weight = modes_here.pop()
    partner = swapped(states[0])

    every = tuple(range(spans))
    deltas = [None] * spans
    later_sums = [[]] * spans
    for stage in range(sections):
        last_stage = stage + 1 == sections
        gates = []
        before = []
        for span in every:
            got = gate(
                meta, base, deltas[span], norm_gain, modes_here, taps, weight, first_sums,
                later_sums[span], [states, partner], before, span,
            )
            gates.append(got[0])
            before = list(got[1:])
        acc = None
        moving = list(gates)
        results = []
        steps = tensors if small_ring else 1
        for k in range(steps):
            final = k + 1 == steps
            if small_ring:
                step = k
                crossed = []
                for span in every:
                    crossed.append(swapped(moving[span]))
                pairs = [list(moving), crossed]
                if not final:
                    for span in every:
                        moving[span] = along_ring(moving[span], 1)
            else:
                step = None
                pairs = [[lax.all_gather(g, ("tensor", "seq"), axis=1, tiled=True) for g in gates]]
            if not final:
                acc = mix("part", meta, step, pairs, every, weight, acc, None, None, seqs, tensors)
                continue
            for span in every:
                kind = "hop" if not last_stage else "out" if span + 1 == spans else "done"
                done = tuple(results) if kind == "out" else ()
                results.append(
                    mix(
                        kind, meta, step, [[part[span]] for part in pairs], (span,), weight,
                        acc, base, deltas[span], seqs, tensors, done,
                    )
                )
        if not last_stage:
            new_deltas, new_sums = [], []
            for span in every:
                moved, partial = results[span]
                new_deltas.append(to_next(moved))
                both = partial + swapped(partial)
                if small_ring:
                    bits = tensors.bit_length() - 1
                    for bit in range(bits - 1):
                        both = both + across(both, 1 << bit)
                    got = []
                    for k in range(2):
                        got.append(to_next_across(both, k * tensors // 2))
                    new_sums.append(got)
                else:
                    new_sums.append([to_next(lax.psum(both, "tensor"))])
            deltas, later_sums = new_deltas, new_sums
    return results[-1]


def solution(mesh):
    placed = (
        P("groups", None),
        P("groups"),
        P(None, "tensor"),
        P("section", "tensor"),
        P("section", None, "tensor"),
        P("section", None, "tensor"),
        P("section", "seq", "groups", "tensor"),
        P("section", None, ("tensor", "seq")),
    )
    return jax.shard_map(
        local,
        mesh=mesh,
        in_specs=placed,
        out_specs=P("section", None, "groups", ("tensor", "seq")),
        check_vma=False,
    )
```

```python
import functools

import jax
import jax.numpy as jnp
from jax import lax
from jax.experimental import pallas as pl
from jax.experimental.pallas import tpu as pltpu
from jax.sharding import PartitionSpec as P


epsilon = 1e-05
highest = lax.Precision.HIGHEST
LANES = 128
SUB = 8
f32 = jnp.float32
MIB = 1 << 20


def params(mib):
    return pltpu.CompilerParams(vmem_limit_bytes=mib * MIB)


def in_vmem(value):
    return pltpu.with_memory_space_constraint(value, pltpu.VMEM)


def row_spread(ref, row, at, lead=()):
    return ref.at[(*lead, slice(None), at)][pl.ds(row, SUB, stride=0), :]


def in_hbm(value):
    return pltpu.with_memory_space_constraint(value, pltpu.HBM)


def cost(flops, moved):
    return pl.CostEstimate(flops=int(flops), bytes_accessed=int(moved), transcendentals=0)


def row_sums(squares):
    ones = jnp.ones((SUB, squares.shape[1]), f32)
    return lax.dot_general(
        ones, squares, (((1,), (1,)), ((), ())), precision=highest, preferred_element_type=f32
    )


def lane_tiles_squared(block):
    total = block[:, :LANES] * block[:, :LANES]
    for start in range(LANES, block.shape[1], LANES):
        piece = block[:, start : start + LANES]
        total = total + piece * piece
    return total


def mode_rows(first, step8, rows, store):
    run = list(first)
    for k in range(rows // SUB):
        total = run[0]
        for q in run[1:]:
            total = total + q
        store(k, total)
        if k + 1 < rows // SUB:
            run = [q * d for q, d in zip(run, step8)]


def spread(values, m):
    return jnp.broadcast_to(values[m : m + 1, :], (SUB, values.shape[1]))


def half_states(side, wide, per_chunk, slot_total, meta, first_span, fetch, held_rows, rates_ref, states):
    slots, rows, half = held_rows.shape
    modes = rates_ref.shape[0]
    rank = meta[0]
    part = 1 - rank if side == 0 else rank

    def one_tile(t, carry):
        @pl.when(lax.rem(t, per_chunk) == 0)
        def _():
            fetch(t // per_chunk).wait()

        at = pl.ds(pl.multiple_of(t * wide, LANES), wide)
        rates = rates_ref[:, pl.ds(pl.multiple_of(part * half + t * wide, LANES), wide)]
        decay = jnp.exp(-rates)
        groups = [decay[g : g + SUB, :] for g in range(0, modes, SUB)]
        held = [[jnp.zeros((SUB, wide), f32) for _ in groups] for _ in range(slots)]
        for r in range(rows):
            for s in range(slots):
                row = row_spread(held_rows, r, at, (s,))
                held[s] = [h * d + row for h, d in zip(held[s], groups)]
        part_a = jnp.zeros((modes, wide), f32)
        part_b = jnp.zeros((modes, wide), f32)
        for s in range(slots):
            slot = rank * slots + s
            age = lax.rem(first_span - slot - 1 + slot_total, slot_total) + 1
            far = (age * rows).astype(f32)
            kept = jnp.where(age < slot_total, 1.0, 0.0).astype(f32)
            total = jnp.concatenate(held[s], axis=0) * decay
            part_a = part_a + total * jnp.exp(-rates * (far - float(rows)))
            part_b = part_b + total * (jnp.exp(-rates * far) * kept)
        states[0, :, at] = part_a
        states[1, :, at] = part_b
        return carry

    lax.fori_loop(0, half // wide, one_tile, 0)


def tile_sizes(half):
    chunk = 512 if half % 512 == 0 else LANES
    return chunk, 2 * LANES if chunk % (2 * LANES) == 0 else LANES


def slot_fetch(side, chunk, meta, cache, held_rows, sems):
    half = held_rows.shape[2]
    part = 1 - meta[0] if side == 0 else meta[0]

    def fetch(j):
        return pltpu.make_async_copy(
            cache.at[:, :, pl.ds(pl.multiple_of(part * half + j * chunk, LANES), chunk)],
            held_rows.at[:, :, pl.ds(pl.multiple_of(j * chunk, LANES), chunk)],
            sems.at[j],
        )

    return fetch


def open_body(pieces, sizes, slot_total, meta, span_any, ids_any, table, cache, rates_any, weight, *rest):
    x_out, sums_out, states, weight_out = rest[:4]
    ids, span_here, words, rows_buf, held_rows, rates_ref, sems, slot_sems = rest[4:]
    chunk, wide = sizes
    spans, rows = sums_out.shape[0], sums_out.shape[2]
    half = x_out.shape[2]
    width = words.shape[1]
    depth = words.shape[0] // pieces
    deep = weight.shape[0] // 2
    fetch = slot_fetch(0, chunk, meta, cache, held_rows, slot_sems)
    small = [
        pltpu.make_async_copy(span_any, span_here, sems.at[pieces]),
        pltpu.make_async_copy(rates_any, rates_ref, sems.at[pieces + 1]),
    ]
    copies = [
        pltpu.make_async_copy(
            table.at[pl.ds(c * depth, depth), :], words.at[pl.ds(c * depth, depth), :], sems.at[c]
        )
        for c in range(pieces)
    ]
    copies.append(pltpu.make_async_copy(ids_any, ids, sems.at[pieces + 2]))
    weight_copy = pltpu.make_async_copy(
        weight.at[pl.ds(0, deep), :], weight_out.at[pl.ds(0, deep), :], sems.at[pieces + 3]
    )
    for copy in small:
        copy.start()
    for j in range(half // chunk):
        fetch(j).start()
    for copy in copies:
        copy.start()
    weight_copy.start()
    for copy in small:
        copy.wait()
    first_span = lax.rem(span_here[0], slot_total)
    half_states(
        0, wide, chunk // wide, slot_total, meta, first_span, fetch, held_rows, rates_ref, states
    )
    for copy in copies:
        copy.wait()
    for span in range(spans):

        def look_up(i, carry, span=span):
            rows_buf[pl.ds(i, 1), :] = words[pl.ds(ids[span, i], 1), :]
            return carry

        lax.fori_loop(0, rows, look_up, 0, unroll=8)
        sums_out[span] = row_sums(lane_tiles_squared(rows_buf[...]))
        for part in range(width // half):

            @pl.when(meta[0] == part)
            def _(part=part, span=span):
                x_out[span] = rows_buf[:, part * half : (part + 1) * half]

    weight_copy.wait()


def open_step(meta, first, ids, table, cache, rates, weight, slot_total):
    spans, rows = ids.shape
    words, width = table.shape
    slots = cache.shape[0]
    modes = rates.shape[0]
    half = weight.shape[1]
    pieces = 4 if words % (4 * SUB) == 0 else 1
    sizes = tile_sizes(half)
    vmem, anywhere = pl.BlockSpec(memory_space=pltpu.VMEM), pl.BlockSpec(memory_space=pl.ANY)
    return pl.pallas_call(
        functools.partial(open_body, pieces, sizes, slot_total),
        out_shape=(
            jax.ShapeDtypeStruct((spans, rows, half), f32),
            jax.ShapeDtypeStruct((spans, SUB, rows), f32),
            jax.ShapeDtypeStruct((2, modes, half), f32),
            pltpu.VMEM(weight.shape, weight.dtype),
        ),
        in_specs=[pl.BlockSpec(memory_space=pltpu.SMEM)] + [anywhere] * 6,
        out_specs=(vmem,) * 4,
        scratch_shapes=[
            pltpu.SMEM((spans, rows), jnp.int32),
            pltpu.SMEM((1,), jnp.int32),
            pltpu.VMEM((words, width), f32),
            pltpu.VMEM((rows, width), f32),
            pltpu.VMEM((slots, rows, half), f32),
            pltpu.VMEM((modes, width), f32),
            pltpu.SemaphoreType.DMA((pieces + 4,)),
            pltpu.SemaphoreType.DMA((half // sizes[0],)),
        ],
        compiler_params=params(10),
        cost_estimate=cost(2 * slots * rows * modes * half, 4 * words * width),
        name="open_step",
    )(meta, first, in_hbm(ids), in_hbm(table), in_hbm(cache), in_hbm(rates), in_hbm(weight))


def history_body(sizes, slot_total, meta, span_any, cache, rates_any, resid_any, weight, held_weight, *rest):
    del held_weight
    states, taps, rates_out, resid_out, weight_out = rest[:5]
    span_here, held_rows, rates_ref, resid_ref, sems, slot_sems = rest[5:]
    chunk, wide = sizes
    _, rows, half = held_rows.shape
    modes = rates_ref.shape[0]
    rank = meta[0]
    deep = weight.shape[0] // 2
    fetch = slot_fetch(1, chunk, meta, cache, held_rows, slot_sems)
    small = [
        pltpu.make_async_copy(span_any, span_here, sems.at[0]),
        pltpu.make_async_copy(rates_any, rates_ref, sems.at[1]),
        pltpu.make_async_copy(resid_any, resid_ref, sems.at[2]),
    ]
    weight_copy = pltpu.make_async_copy(
        weight.at[pl.ds(deep, deep), :], weight_out.at[pl.ds(deep, deep), :], sems.at[3]
    )
    for copy in small:
        copy.start()
    for j in range(half // chunk):
        fetch(j).start()
    weight_copy.start()
    for copy in small:
        copy.wait()
    own = pl.ds(pl.multiple_of(rank * half, LANES), half)
    rates_out[...] = rates_ref[:, own]
    resid_out[...] = resid_ref[:, own]

    def tap_tile(t, carry):
        at = pl.ds(pl.multiple_of(rank * half + t * LANES, LANES), LANES)
        out_at = pl.ds(pl.multiple_of(t * LANES, LANES), LANES)
        rates, resid = rates_ref[:, at], resid_ref[:, at]
        place = lax.broadcasted_iota(jnp.int32, (SUB, LANES), 0).astype(f32)
        step8 = jnp.exp(-rates * float(SUB))
        first = [spread(resid, m) * jnp.exp(-spread(rates, m) * place) for m in range(modes)]

        def store(k, value):
            taps[k * SUB : (k + 1) * SUB, out_at] = value

        mode_rows(first, [spread(step8, m) for m in range(modes)], rows, store)
        return carry

    lax.fori_loop(0, half // LANES, tap_tile, 0)
    first_span = lax.rem(span_here[0], slot_total)
    half_states(
        1, wide, chunk // wide, slot_total, meta, first_span, fetch, held_rows, rates_ref, states
    )
    weight_copy.wait()


def history_states(meta, first, cache, rates, resid, weight, held_weight, slot_total):
    slots, rows, width = cache.shape
    modes = rates.shape[0]
    half = weight.shape[1]
    sizes = tile_sizes(half)
    vmem, anywhere = pl.BlockSpec(memory_space=pltpu.VMEM), pl.BlockSpec(memory_space=pl.ANY)
    return pl.pallas_call(
        functools.partial(history_body, sizes, slot_total),
        out_shape=(
            jax.ShapeDtypeStruct((2, modes, half), f32),
            jax.ShapeDtypeStruct((rows, half), f32),
            jax.ShapeDtypeStruct((modes, half), f32),
            jax.ShapeDtypeStruct((modes, half), f32),
            pltpu.VMEM(weight.shape, weight.dtype),
        ),
        in_specs=[pl.BlockSpec(memory_space=pltpu.SMEM)] + [anywhere] * 6,
        out_specs=(vmem,) * 5,
        scratch_shapes=[
            pltpu.SMEM((1,), jnp.int32),
            pltpu.VMEM((slots, rows, half), f32),
            pltpu.VMEM((modes, width), f32),
            pltpu.VMEM((modes, width), f32),
            pltpu.SemaphoreType.DMA((4,)),
            pltpu.SemaphoreType.DMA((half // sizes[0],)),
        ],
        input_output_aliases={6: 4},
        compiler_params=params(6),
        cost_estimate=cost(2 * slots * rows * modes * half, 4 * slots * rows * half),
        name="history_states",
    )(
        meta, first, in_hbm(cache), in_hbm(rates), in_hbm(resid), in_hbm(weight),
        in_vmem(held_weight),
    )


def gate_body(channels, span, counts, meta, base, *rest):
    n_delta, n_first, n_later, n_before, n_out = counts
    rest = list(rest)

    def take(n):
        return [rest.pop(0) for _ in range(n)]

    delta = take(n_delta)
    gain, rates_ref, resid_ref, taps, mine, theirs = take(6)
    take(1)
    first_sums, later_sums, before = take(n_first), take(n_later), take(n_before)
    gated = rest.pop(0)
    normed_out = take(n_out)
    padded, state_buf = rest
    rows, half = gated.shape
    modes = rates_ref.shape[0]
    blocks = rows // SUB
    is_first = meta[1] == 1
    wide = 4 * LANES if half % (4 * LANES) == 0 else LANES

    if n_before:

        def chain(t, carry):
            at = pl.ds(pl.multiple_of(t * wide, LANES), wide)
            decay = jnp.exp(-rates_ref[:, at])
            groups = [decay[g : g + SUB, :] for g in range(0, modes, SUB)]
            held = [jnp.zeros((SUB, wide), f32) for _ in groups]
            for r in range(rows):
                row = row_spread(before[0], r, at)
                held = [h * d + row for h, d in zip(held, groups)]
            state_buf[:, at] = jnp.concatenate(held, axis=0) * decay + (
                mine[span, :, at] + theirs[span, :, at]
            )
            return carry

        lax.fori_loop(0, half // wide, chain, 0)
    else:
        state_buf[...] = mine[span] + theirs[span]

    sums = first_sums[0][span, 0:1, :]
    for ref in first_sums[1:]:
        sums = sums + ref[span, 0:1, :]
    if n_later:
        later = later_sums[0][span, 0:1, :]
        for ref in later_sums[1:]:
            later = later + ref[span, 0:1, :]
        sums = jnp.where(is_first, sums, later)
    here = lax.broadcasted_iota(jnp.int32, (rows, rows), 0)
    there = lax.broadcasted_iota(jnp.int32, (rows, rows), 1)
    column = jnp.sum(
        jnp.where(here == there, jnp.broadcast_to(sums, (rows, rows)), 0.0), axis=1, keepdims=True
    )
    scale = jnp.broadcast_to(lax.rsqrt(column / float(channels) + epsilon), (rows, LANES))
    padded[0:SUB, :] = jnp.zeros((SUB, LANES), f32)

    def tile(t, carry):
        at = pl.ds(pl.multiple_of(t * LANES, LANES), LANES)
        own = pl.ds(pl.multiple_of(meta[0] * half + t * LANES, LANES), LANES)
        current = base[span, :, at]
        if n_delta:
            current = current + jnp.where(is_first, 0.0, delta[0][:, at].astype(f32))
        normed = current * scale * gain[:, own]
        padded[SUB:, :] = normed
        if n_out:
            normed_out[0][:, at] = normed
        rates = rates_ref[:, at]
        weighted = resid_ref[:, at] * state_buf[:, at]
        step8 = jnp.exp(-rates * float(SUB))
        place = lax.broadcasted_iota(jnp.int32, (SUB, LANES), 0).astype(f32)
        first = [spread(weighted, m) * jnp.exp(-spread(rates, m) * place) for m in range(modes)]
        total = [None] * blocks

        def store(k, value):
            total[k] = value

        mode_rows(first, [spread(step8, m) for m in range(modes)], rows, store)
        for b in range(SUB):
            shifted = [
                padded[SUB + k * SUB - b : 2 * SUB + k * SUB - b, :] for k in range(blocks)
            ]
            for a in range(blocks):
                j = a * SUB + b
                tap = row_spread(taps, j, at)
                for k in range(a, blocks):
                    total[k] = total[k] + tap * shifted[k - a]
        for k in range(blocks):
            rows_at = pl.ds(SUB + k * SUB, SUB)
            gated[k * SUB : (k + 1) * SUB, at] = (padded[rows_at, :] * total[k]).astype(gated.dtype)
        return carry

    lax.fori_loop(0, half // LANES, tile, 0)


def gate(meta, base, delta, gain, modes_here, taps, weight, first_sums, later_sums, states, before, span):
    spans, rows, half = base.shape
    modes = modes_here[0].shape[0]
    vmem = pl.BlockSpec(memory_space=pltpu.VMEM)
    deltas = [] if delta is None else [delta]
    want = int(span + 1 < spans)
    head = [base, *deltas, gain, *modes_here, taps, *states]
    operands = [*head, in_vmem(weight), *first_sums, *later_sums, *before]
    in_specs = [vmem] * len(operands)
    in_specs[len(head)] = pl.BlockSpec(memory_space=pl.ANY)
    counts = (len(deltas), len(first_sums), len(later_sums), len(before), want)
    out_shape = [jax.ShapeDtypeStruct((rows, half), jnp.bfloat16)]
    if want:
        out_shape.append(jax.ShapeDtypeStruct((rows, half), f32))
    return pl.pallas_call(
        functools.partial(gate_body, weight.shape[0], span, counts),
        out_shape=tuple(out_shape),
        in_specs=[pl.BlockSpec(memory_space=pltpu.SMEM)] + in_specs,
        out_specs=tuple(vmem for _ in out_shape),
        scratch_shapes=[pltpu.VMEM((rows + SUB, LANES), f32), pltpu.VMEM((modes, half), f32)],
        compiler_params=params(2),
        cost_estimate=cost(rows * rows * half + 4 * modes * rows * half, 12 * rows * half),
        name="gate",
    )(meta, *operands)


def source_of(step, rank, count):
    place = jnp.where(lax.rem(rank, 2) == 1, (rank + 1) // 2, lax.rem(count - rank // 2, count))
    came = lax.rem(place - step + count, count)
    return jnp.where(came <= count // 2, jnp.maximum(2 * came - 1, 0), 2 * (count - came))


def mix_body(kind, chosen, counts, out_tile, step, own, meta, *refs):
    parts, n_acc, n_base, n_delta, n_done, seqs, tensors = counts
    refs = list(refs)

    def take(n):
        return [refs.pop(0) for _ in range(n)]

    pieces = [take(len(chosen)) for _ in range(parts)]
    (weight,) = take(1)
    acc_in, base, delta, done = take(n_acc), take(n_base), take(n_delta), take(n_done)
    rows, depth = pieces[0][0].shape
    out = weight.shape[1]
    if step is None:
        starts = [0] * parts
    else:
        source = source_of(step, meta[2], tensors) * seqs
        starts = [
            pl.multiple_of((source + (meta[0] if mine else seqs - 1 - meta[0])) * depth, depth)
            for mine in own
        ]
    span = chosen[0]
    squares = jnp.zeros((rows, LANES), f32)
    leaving = []
    if kind == "out":
        fresh_buf, sems = refs[1:]
        for i, ref in enumerate(done):
            leaving.append(pltpu.make_async_copy(ref, refs[0].at[0, i], sems.at[i]))
            leaving[-1].start()
    for n in range(out // out_tile):
        at = slice(n * out_tile, (n + 1) * out_tile)
        total = None
        for p in range(parts):
            lhs = jnp.concatenate([piece[...] for piece in pieces[p]], axis=0)
            more = jnp.dot(lhs, weight[pl.ds(starts[p], depth), at], preferred_element_type=f32)
            total = more if total is None else total + more
        if n_acc and acc_in[0].shape[0] == total.shape[0]:
            total = total + acc_in[0][:, at]
        elif n_acc:
            total = total + acc_in[0][span * rows : (span + 1) * rows, at]
        if kind == "part":
            refs[0][:, at] = total
            continue
        if n_delta:
            total = total + jnp.where(meta[1] == 1, 0.0, delta[0][:, at].astype(f32))
        fresh = base[0][span, :, at] + total
        if kind == "hop":
            refs[0][:, at] = total.astype(refs[0].dtype)
            squares = squares + lane_tiles_squared(fresh)
        elif kind == "done":
            refs[0][:, at] = fresh
        else:
            fresh_buf[:, at] = fresh
            leaving.append(
                pltpu.make_async_copy(
                    fresh_buf.at[:, at], refs[0].at[0, span, :, at], sems.at[len(done) + n]
                )
            )
            leaving[-1].start()
    for copy in leaving:
        copy.wait()
    if kind == "hop":
        for ref in done:
            refs[1][0:span] = ref[0:span]
        refs[1][span] = row_sums(squares)


def mix(kind, meta, step, own, pieces, chosen, weight, acc, base, delta, seqs, tensors, done=()):
    rows, depth = pieces[0][0].shape
    out = weight.shape[1]
    vmem = pl.BlockSpec(memory_space=pltpu.VMEM)
    accs = [] if acc is None else [acc]
    bases = [] if kind == "part" else [base]
    deltas = [] if kind == "part" or delta is None else [delta]
    flat = [piece for part in pieces for piece in part]
    operands = [*flat, in_vmem(weight), *accs, *bases, *deltas, *done]
    counts = (len(pieces), len(accs), len(bases), len(deltas), len(done), seqs, tensors)
    whole = jax.ShapeDtypeStruct((rows * len(chosen), out), f32)
    out_shape, out_specs = whole, vmem
    if kind == "hop":
        out_shape = (
            jax.ShapeDtypeStruct((rows, out), jnp.bfloat16),
            jax.ShapeDtypeStruct((base.shape[0], SUB, rows), f32),
        )
        out_specs = (vmem, vmem)
    elif kind == "out":
        out_shape = jax.ShapeDtypeStruct((1, len(done) + 1, rows, out), f32)
        out_specs = pl.BlockSpec(memory_space=pl.ANY)
    out_tile = 4 * LANES if out % (4 * LANES) == 0 else LANES
    scratch = []
    if kind == "out":
        scratch = [
            pltpu.VMEM((rows, out), f32),
            pltpu.SemaphoreType.DMA((len(done) + out // out_tile,)),
        ]
    return pl.pallas_call(
        functools.partial(mix_body, kind, chosen, counts, out_tile, step, own),
        out_shape=out_shape,
        in_specs=[pl.BlockSpec(memory_space=pltpu.SMEM)] + [vmem] * len(operands),
        out_specs=out_specs,
        scratch_shapes=scratch,
        compiler_params=params(8),
        cost_estimate=cost(
            2 * rows * len(chosen) * depth * out * len(pieces), 2 * depth * out * len(pieces)
        ),
    )(meta, *operands)


def ring_fits(tensors):
    return tensors in (2, 4, 8)


def ring_order(count):
    return list(range(0, 1)) + list(range(1, count, 2)) + list(range(2, count, 2))[::-1]


def local(token_ids, leading_span_index, embed_table, norm_gain, decay_rates, residues, history, mix_weight):
    section_rank = lax.axis_index("section")
    sections = lax.axis_size("section")
    seq_rank = lax.axis_index("seq")
    seqs = lax.axis_size("seq")
    tensor_rank = lax.axis_index("tensor")
    tensors = lax.axis_size("tensor")
    rates, resid, cache, weight = decay_rates[0], residues[0], history[0], mix_weight[0]
    spans, _ = token_ids.shape
    slots, _, _ = cache.shape
    slot_total = slots * seqs
    order = ring_order(tensors)

    def along_ring(value, shift):
        return lax.ppermute(
            value, "tensor", [(order[i], order[(i + shift) % tensors]) for i in range(tensors)]
        )

    def swapped(value):
        return lax.ppermute(value, "seq", [(i, seqs - 1 - i) for i in range(seqs)])

    def to_next(value):
        return lax.ppermute(value, "section", [(i, (i + 1) % sections) for i in range(sections)])

    def across(value, flip):
        return lax.ppermute(value, "tensor", [(i, i ^ flip) for i in range(tensors)])

    def to_next_across(value, flip):
        route = []
        for i in range(tensors):
            for s in range(sections):
                route.append((i * sections + s, (i ^ flip) * sections + (s + 1) % sections))
        return lax.ppermute(value, ("tensor", "section"), route)

    is_first = (section_rank == 0).astype(jnp.int32)
    meta = jnp.stack([seq_rank, is_first, tensor_rank]).astype(jnp.int32)

    base, sums, for_partner, held_weight = open_step(
        meta, leading_span_index, token_ids, embed_table, cache, rates, weight, slot_total
    )
    small_ring = ring_fits(tensors)
    first_sums = [sums]
    if small_ring:
        for k in range(1, tensors):
            first_sums.append(along_ring(sums, k))
    else:
        first_sums = [lax.psum(sums, "tensor")]
    partner = swapped(for_partner)
    states, taps, *modes_here, weight = history_states(
        meta, leading_span_index, cache, rates, resid, weight, held_weight, slot_total
    )

    every = tuple(range(spans))
    deltas = [None] * spans
    later_sums = []
    for stage in range(sections):
        last_stage = stage + 1 == sections
        gates = []
        before = []
        for span in every:
            got = gate(
                meta, base, deltas[span], norm_gain, modes_here, taps, weight, first_sums,
                later_sums, [states, partner], before, span,
            )
            gates.append(got[0])
            before = list(got[1:])
        acc = None
        moving = list(gates)
        results = []
        steps = tensors if small_ring else 1
        for k in range(steps):
            final = k + 1 == steps
            if small_ring:
                step = k
                crossed = []
                for span in every:
                    crossed.append(swapped(moving[span]))
                pairs = [list(moving), crossed]
                if not final:
                    for span in every:
                        moving[span] = along_ring(moving[span], 1)
            else:
                step = None
                pairs = [[lax.all_gather(g, ("tensor", "seq"), axis=1, tiled=True) for g in gates]]
            if not final:
                acc = mix(
                    "part", meta, step, (True, False), pairs, every, weight, acc, None, None,
                    seqs, tensors,
                )
                continue
            for span in every:
                kind = "hop" if not last_stage else "out" if span + 1 == spans else "done"
                done = ()
                if kind == "out":
                    done = tuple(results)
                elif kind == "hop" and span > 0:
                    done = (results[-1][1],)
                acc_here, rest = acc, [[part[span]] for part in pairs]
                own = (True, False)[: len(rest)]
                if small_ring:
                    acc_here = mix(
                        "part", meta, step, own[:1], rest[:1], (span,), weight, acc, None, None,
                        seqs, tensors,
                    )
                    own, rest = own[1:], rest[1:]
                results.append(
                    mix(
                        kind, meta, step, own, rest, (span,), weight, acc_here, base,
                        deltas[span], seqs, tensors, done,
                    )
                )
        if not last_stage:
            deltas = []
            for span in every:
                deltas.append(to_next(results[span][0]))
            both = results[-1][1]
            both = both + swapped(both)
            if small_ring:
                for bit in range(tensors.bit_length() - 2):
                    both = both + across(both, 1 << bit)
                later_sums = []
                for k in range(2):
                    later_sums.append(to_next_across(both, k * tensors // 2))
            else:
                later_sums = [to_next(lax.psum(both, "tensor"))]
    return results[-1]


def solution(mesh):
    placed = (
        P("groups", None),
        P("groups"),
        P(None, "tensor"),
        P("section", "tensor"),
        P("section", None, "tensor"),
        P("section", None, "tensor"),
        P("section", "seq", "groups", "tensor"),
        P("section", None, ("tensor", "seq")),
    )
    return jax.shard_map(
        local,
        mesh=mesh,
        in_specs=placed,
        out_specs=P("section", None, "groups", ("tensor", "seq")),
        check_vma=False,
    )
```

```python
import functools

import jax
import jax.numpy as jnp
from jax import lax
from jax.experimental import pallas as pl
from jax.experimental.pallas import tpu as pltpu
from jax.sharding import PartitionSpec as P


epsilon = 1e-05
highest = lax.Precision.HIGHEST
LANES = 128
SUB = 8
f32 = jnp.float32
MIB = 1 << 20


def params(mib):
    return pltpu.CompilerParams(vmem_limit_bytes=mib * MIB)


def in_vmem(value):
    return pltpu.with_memory_space_constraint(value, pltpu.VMEM)


def row_spread(ref, row, at, lead=()):
    return ref.at[(*lead, slice(None), at)][pl.ds(row, SUB, stride=0), :]


def in_hbm(value):
    return pltpu.with_memory_space_constraint(value, pltpu.HBM)


def cost(flops, moved):
    return pl.CostEstimate(flops=int(flops), bytes_accessed=int(moved), transcendentals=0)


def row_sums(squares):
    ones = jnp.ones((SUB, squares.shape[1]), f32)
    return lax.dot_general(
        ones, squares, (((1,), (1,)), ((), ())), precision=highest, preferred_element_type=f32
    )


def lane_tiles_squared(block):
    total = block[:, :LANES] * block[:, :LANES]
    for start in range(LANES, block.shape[1], LANES):
        piece = block[:, start : start + LANES]
        total = total + piece * piece
    return total


def mode_rows(first, step8, rows, store):
    run = list(first)
    for k in range(rows // SUB):
        total = run[0]
        for q in run[1:]:
            total = total + q
        store(k, total)
        if k + 1 < rows // SUB:
            run = [q * d for q, d in zip(run, step8)]


def spread(values, m):
    return jnp.broadcast_to(values[m : m + 1, :], (SUB, values.shape[1]))


def half_states(side, wide, per_chunk, slot_total, meta, first_span, fetch, held_rows, rates_ref, states):
    slots, rows, half = held_rows.shape
    modes = rates_ref.shape[0]
    rank = meta[0]
    part = 1 - rank if side == 0 else rank

    def one_tile(t, carry):
        @pl.when(lax.rem(t, per_chunk) == 0)
        def _():
            fetch(t // per_chunk).wait()

        at = pl.ds(pl.multiple_of(t * wide, LANES), wide)
        rates = rates_ref[:, pl.ds(pl.multiple_of(part * half + t * wide, LANES), wide)]
        decay = jnp.exp(-rates)
        groups = [decay[g : g + SUB, :] for g in range(0, modes, SUB)]
        held = [[jnp.zeros((SUB, wide), f32) for _ in groups] for _ in range(slots)]
        for r in range(rows):
            for s in range(slots):
                row = row_spread(held_rows, r, at, (s,))
                held[s] = [h * d + row for h, d in zip(held[s], groups)]
        part_a = jnp.zeros((modes, wide), f32)
        part_b = jnp.zeros((modes, wide), f32)
        for s in range(slots):
            slot = rank * slots + s
            age = lax.rem(first_span - slot - 1 + slot_total, slot_total) + 1
            far = (age * rows).astype(f32)
            kept = jnp.where(age < slot_total, 1.0, 0.0).astype(f32)
            total = jnp.concatenate(held[s], axis=0) * decay
            part_a = part_a + total * jnp.exp(-rates * (far - float(rows)))
            part_b = part_b + total * (jnp.exp(-rates * far) * kept)
        states[0, :, at] = part_a
        states[1, :, at] = part_b
        return carry

    lax.fori_loop(0, half // wide, one_tile, 0)


def tile_sizes(half):
    chunk = 512 if half % 512 == 0 else LANES
    return chunk, 2 * LANES if chunk % (2 * LANES) == 0 else LANES


def slot_fetch(side, chunk, meta, cache, held_rows, sems):
    half = held_rows.shape[2]
    part = 1 - meta[0] if side == 0 else meta[0]

    def fetch(j):
        return pltpu.make_async_copy(
            cache.at[:, :, pl.ds(pl.multiple_of(part * half + j * chunk, LANES), chunk)],
            held_rows.at[:, :, pl.ds(pl.multiple_of(j * chunk, LANES), chunk)],
            sems.at[j],
        )

    return fetch


def open_body(pieces, sizes, slot_total, meta, span_any, ids_any, table, cache, rates_any, weight, *rest):
    x_out, sums_out, states, weight_out = rest[:4]
    ids, span_here, words, rows_buf, held_rows, rates_ref, sems, slot_sems = rest[4:]
    chunk, wide = sizes
    spans, rows = sums_out.shape[0], sums_out.shape[2]
    half = x_out.shape[2]
    width = words.shape[1]
    depth = words.shape[0] // pieces
    deep = weight.shape[0] // 2
    fetch = slot_fetch(0, chunk, meta, cache, held_rows, slot_sems)
    small = [
        pltpu.make_async_copy(span_any, span_here, sems.at[pieces]),
        pltpu.make_async_copy(rates_any, rates_ref, sems.at[pieces + 1]),
    ]
    copies = [
        pltpu.make_async_copy(
            table.at[pl.ds(c * depth, depth), :], words.at[pl.ds(c * depth, depth), :], sems.at[c]
        )
        for c in range(pieces)
    ]
    copies.append(pltpu.make_async_copy(ids_any, ids, sems.at[pieces + 2]))
    weight_copy = pltpu.make_async_copy(
        weight.at[pl.ds(0, deep), :], weight_out.at[pl.ds(0, deep), :], sems.at[pieces + 3]
    )
    for copy in small:
        copy.start()
    for j in range(half // chunk):
        fetch(j).start()
    for copy in copies:
        copy.start()
    weight_copy.start()
    for copy in small:
        copy.wait()
    first_span = lax.rem(span_here[0], slot_total)
    half_states(
        0, wide, chunk // wide, slot_total, meta, first_span, fetch, held_rows, rates_ref, states
    )
    for copy in copies:
        copy.wait()
    for span in range(spans):

        def look_up(i, carry, span=span):
            rows_buf[pl.ds(i, 1), :] = words[pl.ds(ids[span, i], 1), :]
            return carry

        lax.fori_loop(0, rows, look_up, 0, unroll=8)
        sums_out[span] = row_sums(lane_tiles_squared(rows_buf[...]))
        for part in range(width // half):

            @pl.when(meta[0] == part)
            def _(part=part, span=span):
                x_out[span] = rows_buf[:, part * half : (part + 1) * half]

    weight_copy.wait()


def open_step(meta, first, ids, table, cache, rates, weight, slot_total):
    spans, rows = ids.shape
    words, width = table.shape
    slots = cache.shape[0]
    modes = rates.shape[0]
    half = weight.shape[1]
    pieces = 4 if words % (4 * SUB) == 0 else 1
    sizes = tile_sizes(half)
    vmem, anywhere = pl.BlockSpec(memory_space=pltpu.VMEM), pl.BlockSpec(memory_space=pl.ANY)
    return pl.pallas_call(
        functools.partial(open_body, pieces, sizes, slot_total),
        out_shape=(
            jax.ShapeDtypeStruct((spans, rows, half), f32),
            jax.ShapeDtypeStruct((spans, SUB, rows), f32),
            jax.ShapeDtypeStruct((2, modes, half), f32),
            pltpu.VMEM(weight.shape, weight.dtype),
        ),
        in_specs=[pl.BlockSpec(memory_space=pltpu.SMEM)] + [anywhere] * 6,
        out_specs=(vmem,) * 4,
        scratch_shapes=[
            pltpu.SMEM((spans, rows), jnp.int32),
            pltpu.SMEM((1,), jnp.int32),
            pltpu.VMEM((words, width), f32),
            pltpu.VMEM((rows, width), f32),
            pltpu.VMEM((slots, rows, half), f32),
            pltpu.VMEM((modes, width), f32),
            pltpu.SemaphoreType.DMA((pieces + 4,)),
            pltpu.SemaphoreType.DMA((half // sizes[0],)),
        ],
        compiler_params=params(10),
        cost_estimate=cost(2 * slots * rows * modes * half, 4 * words * width),
        name="open_step",
    )(meta, first, in_hbm(ids), in_hbm(table), in_hbm(cache), in_hbm(rates), in_hbm(weight))


def history_body(sizes, slot_total, meta, span_any, cache, rates_any, resid_any, weight, held_weight, *rest):
    del held_weight
    states, taps, rates_out, resid_out, weight_out = rest[:5]
    span_here, held_rows, rates_ref, resid_ref, sems, slot_sems = rest[5:]
    chunk, wide = sizes
    _, rows, half = held_rows.shape
    modes = rates_ref.shape[0]
    rank = meta[0]
    deep = weight.shape[0] // 2
    fetch = slot_fetch(1, chunk, meta, cache, held_rows, slot_sems)
    small = [
        pltpu.make_async_copy(span_any, span_here, sems.at[0]),
        pltpu.make_async_copy(rates_any, rates_ref, sems.at[1]),
        pltpu.make_async_copy(resid_any, resid_ref, sems.at[2]),
    ]
    weight_copy = pltpu.make_async_copy(
        weight.at[pl.ds(deep, deep), :], weight_out.at[pl.ds(deep, deep), :], sems.at[3]
    )
    for copy in small:
        copy.start()
    for j in range(half // chunk):
        fetch(j).start()
    weight_copy.start()
    for copy in small:
        copy.wait()
    own = pl.ds(pl.multiple_of(rank * half, LANES), half)
    rates_out[...] = rates_ref[:, own]
    resid_out[...] = resid_ref[:, own]

    def tap_tile(t, carry):
        at = pl.ds(pl.multiple_of(rank * half + t * LANES, LANES), LANES)
        out_at = pl.ds(pl.multiple_of(t * LANES, LANES), LANES)
        rates, resid = rates_ref[:, at], resid_ref[:, at]
        place = lax.broadcasted_iota(jnp.int32, (SUB, LANES), 0).astype(f32)
        step8 = jnp.exp(-rates * float(SUB))
        first = [spread(resid, m) * jnp.exp(-spread(rates, m) * place) for m in range(modes)]

        def store(k, value):
            taps[k * SUB : (k + 1) * SUB, out_at] = value

        mode_rows(first, [spread(step8, m) for m in range(modes)], rows, store)
        return carry

    lax.fori_loop(0, half // LANES, tap_tile, 0)
    first_span = lax.rem(span_here[0], slot_total)
    half_states(
        1, wide, chunk // wide, slot_total, meta, first_span, fetch, held_rows, rates_ref, states
    )
    weight_copy.wait()


def history_states(meta, first, cache, rates, resid, weight, held_weight, slot_total):
    slots, rows, width = cache.shape
    modes = rates.shape[0]
    half = weight.shape[1]
    sizes = tile_sizes(half)
    vmem, anywhere = pl.BlockSpec(memory_space=pltpu.VMEM), pl.BlockSpec(memory_space=pl.ANY)
    return pl.pallas_call(
        functools.partial(history_body, sizes, slot_total),
        out_shape=(
            jax.ShapeDtypeStruct((2, modes, half), f32),
            jax.ShapeDtypeStruct((rows, half), f32),
            jax.ShapeDtypeStruct((modes, half), f32),
            jax.ShapeDtypeStruct((modes, half), f32),
            pltpu.VMEM(weight.shape, weight.dtype),
        ),
        in_specs=[pl.BlockSpec(memory_space=pltpu.SMEM)] + [anywhere] * 6,
        out_specs=(vmem,) * 5,
        scratch_shapes=[
            pltpu.SMEM((1,), jnp.int32),
            pltpu.VMEM((slots, rows, half), f32),
            pltpu.VMEM((modes, width), f32),
            pltpu.VMEM((modes, width), f32),
            pltpu.SemaphoreType.DMA((4,)),
            pltpu.SemaphoreType.DMA((half // sizes[0],)),
        ],
        input_output_aliases={6: 4},
        compiler_params=params(6),
        cost_estimate=cost(2 * slots * rows * modes * half, 4 * slots * rows * half),
        name="history_states",
    )(
        meta, first, in_hbm(cache), in_hbm(rates), in_hbm(resid), in_hbm(weight),
        in_vmem(held_weight),
    )


def gate_body(channels, span, counts, meta, base, *rest):
    n_delta, n_first, n_later, n_before, n_past, n_out, n_keep = counts
    rest = list(rest)

    def take(n):
        return [rest.pop(0) for _ in range(n)]

    delta = take(n_delta)
    gain, rates_ref, resid_ref, taps, mine, theirs = take(6)
    take(1)
    first_sums, later_sums, before = take(n_first), take(n_later), take(n_before)
    past = take(n_past)
    gated = rest.pop(0)
    normed_out, past_out = take(n_out), take(n_keep)
    padded, state_buf = rest
    rows, half = gated.shape
    modes = rates_ref.shape[0]
    blocks = rows // SUB
    is_first = meta[1] == 1
    wide = 4 * LANES if half % (4 * LANES) == 0 else LANES

    if n_before:

        def chain(t, carry):
            at = pl.ds(pl.multiple_of(t * wide, LANES), wide)
            decay = jnp.exp(-rates_ref[:, at])
            groups = [decay[g : g + SUB, :] for g in range(0, modes, SUB)]
            held = [jnp.zeros((SUB, wide), f32) for _ in groups]
            for r in range(rows):
                row = row_spread(before[0], r, at)
                held = [h * d + row for h, d in zip(held, groups)]
            state_buf[:, at] = jnp.concatenate(held, axis=0) * decay + (
                mine[span, :, at] + theirs[span, :, at]
            )
            return carry

        lax.fori_loop(0, half // wide, chain, 0)
    elif not n_past:
        state_buf[...] = mine[span] + theirs[span]

    sums = first_sums[0][span, 0:1, :]
    for ref in first_sums[1:]:
        sums = sums + ref[span, 0:1, :]
    if n_later:
        later = later_sums[0][span, 0:1, :]
        for ref in later_sums[1:]:
            later = later + ref[span, 0:1, :]
        sums = jnp.where(is_first, sums, later)
    here = lax.broadcasted_iota(jnp.int32, (rows, rows), 0)
    there = lax.broadcasted_iota(jnp.int32, (rows, rows), 1)
    column = jnp.sum(
        jnp.where(here == there, jnp.broadcast_to(sums, (rows, rows)), 0.0), axis=1, keepdims=True
    )
    scale = jnp.broadcast_to(lax.rsqrt(column / float(channels) + epsilon), (rows, LANES))
    padded[0:SUB, :] = jnp.zeros((SUB, LANES), f32)

    def tile(t, carry):
        at = pl.ds(pl.multiple_of(t * LANES, LANES), LANES)
        own = pl.ds(pl.multiple_of(meta[0] * half + t * LANES, LANES), LANES)
        current = base[span, :, at]
        if n_delta:
            current = current + jnp.where(is_first, 0.0, delta[0][:, at].astype(f32))
        normed = current * scale * gain[:, own]
        padded[SUB:, :] = normed
        if n_out:
            normed_out[0][:, at] = normed
        rates = rates_ref[:, at]
        total = [None] * blocks

        def store(k, value):
            total[k] = value

        if n_past:
            for k in range(blocks):
                total[k] = past[0][k * SUB : (k + 1) * SUB, at]
        else:
            weighted = resid_ref[:, at] * state_buf[:, at]
            step8 = jnp.exp(-rates * float(SUB))
            place = lax.broadcasted_iota(jnp.int32, (SUB, LANES), 0).astype(f32)
            first = [spread(weighted, m) * jnp.exp(-spread(rates, m) * place) for m in range(modes)]
            mode_rows(first, [spread(step8, m) for m in range(modes)], rows, store)
            if n_keep:
                for k in range(blocks):
                    past_out[0][k * SUB : (k + 1) * SUB, at] = total[k]
        for b in range(SUB):
            shifted = [
                padded[SUB + k * SUB - b : 2 * SUB + k * SUB - b, :] for k in range(blocks)
            ]
            for a in range(blocks):
                tap = row_spread(taps, a * SUB + b, at)
                for k in range(a, blocks):
                    total[k] = total[k] + tap * shifted[k - a]
        for k in range(blocks):
            block = padded[pl.ds(SUB + k * SUB, SUB), :]
            gated[k * SUB : (k + 1) * SUB, at] = (block * total[k]).astype(gated.dtype)
        return carry

    lax.fori_loop(0, half // LANES, tile, 0)


def gate(meta, base, delta, gain, modes_here, taps, weight, first_sums, later_sums, states, before, past, keep, span):
    spans, rows, half = base.shape
    modes = modes_here[0].shape[0]
    vmem = pl.BlockSpec(memory_space=pltpu.VMEM)
    deltas = [] if delta is None else [delta]
    want = int(span + 1 < spans)
    head = [base, *deltas, gain, *modes_here, taps, *states]
    operands = [*head, in_vmem(weight), *first_sums, *later_sums, *before, *past]
    in_specs = [vmem] * len(operands)
    in_specs[len(head)] = pl.BlockSpec(memory_space=pl.ANY)
    counts = (len(deltas), len(first_sums), len(later_sums), len(before), len(past), want, int(keep))
    out_shape = [jax.ShapeDtypeStruct((rows, half), jnp.bfloat16)]
    if want:
        out_shape.append(jax.ShapeDtypeStruct((rows, half), f32))
    if keep:
        out_shape.append(jax.ShapeDtypeStruct((rows, half), f32))
    return pl.pallas_call(
        functools.partial(gate_body, weight.shape[0], span, counts),
        out_shape=tuple(out_shape),
        in_specs=[pl.BlockSpec(memory_space=pltpu.SMEM)] + in_specs,
        out_specs=tuple(vmem for _ in out_shape),
        scratch_shapes=[pltpu.VMEM((rows + SUB, LANES), f32), pltpu.VMEM((modes, half), f32)],
        compiler_params=params(2),
        cost_estimate=cost(rows * rows * half + 4 * modes * rows * half, 12 * rows * half),
        name="gate",
    )(meta, *operands)


def source_of(step, rank, count):
    place = jnp.where(lax.rem(rank, 2) == 1, (rank + 1) // 2, lax.rem(count - rank // 2, count))
    came = lax.rem(place - step + count, count)
    return jnp.where(came <= count // 2, jnp.maximum(2 * came - 1, 0), 2 * (count - came))


def mix_body(kind, chosen, counts, out_tile, step, own, meta, *refs):
    parts, n_acc, n_base, n_delta, n_done, seqs, tensors = counts
    refs = list(refs)

    def take(n):
        return [refs.pop(0) for _ in range(n)]

    pieces = [take(len(chosen)) for _ in range(parts)]
    (weight,) = take(1)
    acc_in, base, delta, done = take(n_acc), take(n_base), take(n_delta), take(n_done)
    rows, depth = pieces[0][0].shape
    out = weight.shape[1]
    if step is None:
        starts = [0] * parts
    else:
        source = source_of(step, meta[2], tensors) * seqs
        starts = [
            pl.multiple_of((source + (meta[0] if mine else seqs - 1 - meta[0])) * depth, depth)
            for mine in own
        ]
    span = chosen[0]
    squares = jnp.zeros((rows, LANES), f32)
    leaving = []
    if kind == "out":
        fresh_buf, sems = refs[1:]
        for i, ref in enumerate(done):
            leaving.append(pltpu.make_async_copy(ref, refs[0].at[0, i], sems.at[i]))
            leaving[-1].start()
    for n in range(out // out_tile):
        at = slice(n * out_tile, (n + 1) * out_tile)
        total = None
        for p in range(parts):
            lhs = jnp.concatenate([piece[...] for piece in pieces[p]], axis=0)
            more = jnp.dot(lhs, weight[pl.ds(starts[p], depth), at], preferred_element_type=f32)
            total = more if total is None else total + more
        if n_acc and acc_in[0].shape[0] == total.shape[0]:
            total = total + acc_in[0][:, at]
        elif n_acc:
            total = total + acc_in[0][span * rows : (span + 1) * rows, at]
        if kind == "part":
            refs[0][:, at] = total
            continue
        if n_delta:
            total = total + jnp.where(meta[1] == 1, 0.0, delta[0][:, at].astype(f32))
        fresh = base[0][span, :, at] + total
        if kind == "hop":
            refs[0][:, at] = total.astype(refs[0].dtype)
            squares = squares + lane_tiles_squared(fresh)
        elif kind == "done":
            refs[0][:, at] = fresh
        else:
            fresh_buf[:, at] = fresh
            leaving.append(
                pltpu.make_async_copy(
                    fresh_buf.at[:, at], refs[0].at[0, span, :, at], sems.at[len(done) + n]
                )
            )
            leaving[-1].start()
    for copy in leaving:
        copy.wait()
    if kind == "hop":
        for ref in done:
            refs[1][0:span] = ref[0:span]
        refs[1][span] = row_sums(squares)


def mix(kind, meta, step, own, pieces, chosen, weight, acc, base, delta, seqs, tensors, done=()):
    rows, depth = pieces[0][0].shape
    out = weight.shape[1]
    vmem = pl.BlockSpec(memory_space=pltpu.VMEM)
    accs = [] if acc is None else [acc]
    bases = [] if kind == "part" else [base]
    deltas = [] if kind == "part" or delta is None else [delta]
    flat = [piece for part in pieces for piece in part]
    operands = [*flat, in_vmem(weight), *accs, *bases, *deltas, *done]
    counts = (len(pieces), len(accs), len(bases), len(deltas), len(done), seqs, tensors)
    whole = jax.ShapeDtypeStruct((rows * len(chosen), out), f32)
    out_shape, out_specs = whole, vmem
    if kind == "hop":
        out_shape = (
            jax.ShapeDtypeStruct((rows, out), jnp.bfloat16),
            jax.ShapeDtypeStruct((base.shape[0], SUB, rows), f32),
        )
        out_specs = (vmem, vmem)
    elif kind == "out":
        out_shape = jax.ShapeDtypeStruct((1, len(done) + 1, rows, out), f32)
        out_specs = pl.BlockSpec(memory_space=pl.ANY)
    out_tile = 4 * LANES if out % (4 * LANES) == 0 else LANES
    scratch = []
    if kind == "out":
        scratch = [
            pltpu.VMEM((rows, out), f32),
            pltpu.SemaphoreType.DMA((len(done) + out // out_tile,)),
        ]
    return pl.pallas_call(
        functools.partial(mix_body, kind, chosen, counts, out_tile, step, own),
        out_shape=out_shape,
        in_specs=[pl.BlockSpec(memory_space=pltpu.SMEM)] + [vmem] * len(operands),
        out_specs=out_specs,
        scratch_shapes=scratch,
        compiler_params=params(8),
        cost_estimate=cost(
            2 * rows * len(chosen) * depth * out * len(pieces), 2 * depth * out * len(pieces)
        ),
    )(meta, *operands)


def ring_fits(tensors):
    return tensors in (2, 4, 8)


def ring_order(count):
    return list(range(0, 1)) + list(range(1, count, 2)) + list(range(2, count, 2))[::-1]


def local(token_ids, leading_span_index, embed_table, norm_gain, decay_rates, residues, history, mix_weight):
    section_rank = lax.axis_index("section")
    sections = lax.axis_size("section")
    seq_rank = lax.axis_index("seq")
    seqs = lax.axis_size("seq")
    tensor_rank = lax.axis_index("tensor")
    tensors = lax.axis_size("tensor")
    rates, resid, cache, weight = decay_rates[0], residues[0], history[0], mix_weight[0]
    spans, _ = token_ids.shape
    slots, _, _ = cache.shape
    slot_total = slots * seqs
    order = ring_order(tensors)

    def along_ring(value, shift):
        return lax.ppermute(
            value, "tensor", [(order[i], order[(i + shift) % tensors]) for i in range(tensors)]
        )

    def swapped(value):
        return lax.ppermute(value, "seq", [(i, seqs - 1 - i) for i in range(seqs)])

    def to_next(value):
        return lax.ppermute(value, "section", [(i, (i + 1) % sections) for i in range(sections)])

    def across(value, flip):
        return lax.ppermute(value, "tensor", [(i, i ^ flip) for i in range(tensors)])

    def to_next_across(value, flip):
        route = []
        for i in range(tensors):
            for s in range(sections):
                route.append((i * sections + s, (i ^ flip) * sections + (s + 1) % sections))
        return lax.ppermute(value, ("tensor", "section"), route)

    is_first = (section_rank == 0).astype(jnp.int32)
    meta = jnp.stack([seq_rank, is_first, tensor_rank]).astype(jnp.int32)

    base, sums, for_partner, held_weight = open_step(
        meta, leading_span_index, token_ids, embed_table, cache, rates, weight, slot_total
    )
    small_ring = ring_fits(tensors)
    first_sums = [sums]
    if small_ring:
        for k in range(1, tensors):
            first_sums.append(along_ring(sums, k))
    else:
        first_sums = [lax.psum(sums, "tensor")]
    partner = swapped(for_partner)
    states, taps, *modes_here, weight = history_states(
        meta, leading_span_index, cache, rates, resid, weight, held_weight, slot_total
    )

    every = tuple(range(spans))
    deltas = [None] * spans
    later_sums = []
    past = []
    for stage in range(sections):
        last_stage = stage + 1 == sections
        gates = []
        before = []
        for span in every:
            got = gate(
                meta, base, deltas[span], norm_gain, modes_here, taps, weight, first_sums,
                later_sums, [states, partner], before, past if span == 0 else [],
                span == 0 and stage == 0 and not last_stage, span,
            )
            gates.append(got[0])
            before = list(got[1:2])
            if len(got) == 3:
                past = [got[2]]
        acc = None
        moving = list(gates)
        results = []
        steps = tensors if small_ring else 1
        for k in range(steps):
            final = k + 1 == steps
            if small_ring:
                step = k
                crossed = []
                for span in every:
                    crossed.append(swapped(moving[span]))
                pairs = [list(moving), crossed]
                if not final:
                    for span in every:
                        moving[span] = along_ring(moving[span], 1)
            else:
                step = None
                pairs = [[lax.all_gather(g, ("tensor", "seq"), axis=1, tiled=True) for g in gates]]
            if not final:
                acc = mix(
                    "part", meta, step, (True, False), pairs, every, weight, acc, None, None,
                    seqs, tensors,
                )
                continue
            for span in every:
                kind = "hop" if not last_stage else "out" if span + 1 == spans else "done"
                done = ()
                if kind == "out":
                    done = tuple(results)
                elif kind == "hop" and span > 0:
                    done = (results[-1][1],)
                acc_here, rest = acc, [[part[span]] for part in pairs]
                own = (True, False)[: len(rest)]
                if small_ring:
                    acc_here = mix(
                        "part", meta, step, own[:1], rest[:1], (span,), weight, acc, None, None,
                        seqs, tensors,
                    )
                    own, rest = own[1:], rest[1:]
                results.append(
                    mix(
                        kind, meta, step, own, rest, (span,), weight, acc_here, base,
                        deltas[span], seqs, tensors, done,
                    )
                )
        if not last_stage:
            deltas = []
            for span in every:
                deltas.append(to_next(results[span][0]))
            both = results[-1][1]
            both = both + swapped(both)
            if small_ring:
                for bit in range(tensors.bit_length() - 2):
                    both = both + across(both, 1 << bit)
                later_sums = []
                for k in range(2):
                    later_sums.append(to_next_across(both, k * tensors // 2))
            else:
                later_sums = [to_next(lax.psum(both, "tensor"))]
    return results[-1]


def solution(mesh):
    placed = (
        P("groups", None),
        P("groups"),
        P(None, "tensor"),
        P("section", "tensor"),
        P("section", None, "tensor"),
        P("section", None, "tensor"),
        P("section", "seq", "groups", "tensor"),
        P("section", None, ("tensor", "seq")),
    )
    return jax.shard_map(
        local,
        mesh=mesh,
        in_specs=placed,
        out_specs=P("section", None, "groups", ("tensor", "seq")),
        check_vma=False,
    )
```

```python
import functools

import jax
import jax.numpy as jnp
from jax import lax
from jax.experimental import pallas as pl
from jax.experimental.pallas import tpu as pltpu
from jax.sharding import PartitionSpec as P


epsilon = 1e-05
highest = lax.Precision.HIGHEST
LANES = 128
SUB = 8
f32 = jnp.float32
MIB = 1 << 20


def params(mib):
    return pltpu.CompilerParams(vmem_limit_bytes=mib * MIB)


def in_vmem(value):
    return pltpu.with_memory_space_constraint(value, pltpu.VMEM)


def row_spread(ref, row, at, lead=()):
    return ref.at[(*lead, slice(None), at)][pl.ds(row, SUB, stride=0), :]


def in_hbm(value):
    return pltpu.with_memory_space_constraint(value, pltpu.HBM)


def cost(flops, moved):
    return pl.CostEstimate(flops=int(flops), bytes_accessed=int(moved), transcendentals=0)


def row_sums(squares):
    ones = jnp.ones((SUB, squares.shape[1]), f32)
    return lax.dot_general(
        ones, squares, (((1,), (1,)), ((), ())), precision=highest, preferred_element_type=f32
    )


def lane_tiles_squared(block):
    total = block[:, :LANES] * block[:, :LANES]
    for start in range(LANES, block.shape[1], LANES):
        piece = block[:, start : start + LANES]
        total = total + piece * piece
    return total


def mode_rows(first, step8, rows, store):
    run = list(first)
    for k in range(rows // SUB):
        total = run[0]
        for q in run[1:]:
            total = total + q
        store(k, total)
        if k + 1 < rows // SUB:
            run = [q * d for q, d in zip(run, step8)]


def spread(values, m):
    return jnp.broadcast_to(values[m : m + 1, :], (SUB, values.shape[1]))


def half_states(offset, wide, per_chunk, slot_total, meta, first_span, fetch, held_rows, rates_ref, states):
    slots, rows, half = held_rows.shape
    modes = rates_ref.shape[0]
    rank = meta[0]

    def one_tile(t, carry):
        @pl.when(lax.rem(t, per_chunk) == 0)
        def _():
            fetch(t // per_chunk).wait()

        at = pl.ds(pl.multiple_of(t * wide, LANES), wide)
        rates = rates_ref[:, pl.ds(pl.multiple_of(offset + t * wide, LANES), wide)]
        decay = jnp.exp(-rates)
        groups = [decay[g : g + SUB, :] for g in range(0, modes, SUB)]
        held = [[jnp.zeros((SUB, wide), f32) for _ in groups] for _ in range(slots)]
        for r in range(rows):
            for s in range(slots):
                row = row_spread(held_rows, r, at, (s,))
                held[s] = [h * d + row for h, d in zip(held[s], groups)]
        part_a = jnp.zeros((modes, wide), f32)
        part_b = jnp.zeros((modes, wide), f32)
        for s in range(slots):
            slot = rank * slots + s
            age = lax.rem(first_span - slot - 1 + slot_total, slot_total) + 1
            far = (age * rows).astype(f32)
            kept = jnp.where(age < slot_total, 1.0, 0.0).astype(f32)
            total = jnp.concatenate(held[s], axis=0) * decay
            part_a = part_a + total * jnp.exp(-rates * (far - float(rows)))
            part_b = part_b + total * (jnp.exp(-rates * far) * kept)
        states[0, :, at] = part_a
        states[1, :, at] = part_b
        return carry

    lax.fori_loop(0, half // wide, one_tile, 0)


def early_rows(weight):
    return weight.shape[0] // 16 * 10


def tile_sizes(half):
    chunk = 512 if half % 512 == 0 else LANES
    return chunk, 2 * LANES if chunk % (2 * LANES) == 0 else LANES


def slot_fetch(side, chunk, meta, cache, held_rows, sems):
    half = held_rows.shape[2]
    part = 1 - meta[0] if side == 0 else meta[0]

    def fetch(j):
        return pltpu.make_async_copy(
            cache.at[:, :, pl.ds(pl.multiple_of(part * half + j * chunk, LANES), chunk)],
            held_rows.at[:, :, pl.ds(pl.multiple_of(j * chunk, LANES), chunk)],
            sems.at[j],
        )

    return fetch


def open_body(pieces, sizes, slot_total, meta, span_any, ids_any, table, cache, rates_any, resid_any, weight, *rest):
    x_out, sums_out, states, rates_out, resid_out, weight_out = rest[:6]
    ids, span_here, words, rows_buf, held_rows, rates_ref, sems, slot_sems = rest[6:]
    chunk, wide = sizes
    spans, rows = sums_out.shape[0], sums_out.shape[2]
    half = x_out.shape[2]
    width = words.shape[1]
    depth = words.shape[0] // pieces
    deep = early_rows(weight)
    fetch = slot_fetch(0, chunk, meta, cache, held_rows, slot_sems)
    small = [
        pltpu.make_async_copy(span_any, span_here, sems.at[pieces]),
        pltpu.make_async_copy(rates_any, rates_ref, sems.at[pieces + 1]),
    ]
    copies = [
        pltpu.make_async_copy(
            table.at[pl.ds(c * depth, depth), :], words.at[pl.ds(c * depth, depth), :], sems.at[c]
        )
        for c in range(pieces)
    ]
    copies.append(pltpu.make_async_copy(ids_any, ids, sems.at[pieces + 2]))
    own = pl.ds(pl.multiple_of(meta[0] * half, LANES), half)
    copies.append(pltpu.make_async_copy(resid_any.at[:, own], resid_out, sems.at[pieces + 4]))
    weight_copy = pltpu.make_async_copy(
        weight.at[pl.ds(0, deep), :], weight_out.at[pl.ds(0, deep), :], sems.at[pieces + 3]
    )
    for copy in small:
        copy.start()
    for j in range(half // chunk):
        fetch(j).start()
    for copy in copies:
        copy.start()
    weight_copy.start()
    for copy in small:
        copy.wait()
    first_span = lax.rem(span_here[0], slot_total)
    rates_out[...] = rates_ref[:, own]
    half_states(
        (1 - meta[0]) * half, wide, chunk // wide, slot_total, meta, first_span, fetch, held_rows,
        rates_ref, states,
    )
    for copy in copies:
        copy.wait()
    for span in range(spans):

        def look_up(i, carry, span=span):
            rows_buf[pl.ds(i, 1), :] = words[pl.ds(ids[span, i], 1), :]
            return carry

        lax.fori_loop(0, rows, look_up, 0, unroll=8)
        sums_out[span] = row_sums(lane_tiles_squared(rows_buf[...]))
        for part in range(width // half):

            @pl.when(meta[0] == part)
            def _(part=part, span=span):
                x_out[span] = rows_buf[:, part * half : (part + 1) * half]

    weight_copy.wait()


def open_step(meta, first, ids, table, cache, rates, resid, weight, slot_total):
    spans, rows = ids.shape
    words, width = table.shape
    slots = cache.shape[0]
    modes = rates.shape[0]
    half = weight.shape[1]
    pieces = 4 if words % (4 * SUB) == 0 else 1
    sizes = tile_sizes(half)
    vmem, anywhere = pl.BlockSpec(memory_space=pltpu.VMEM), pl.BlockSpec(memory_space=pl.ANY)
    return pl.pallas_call(
        functools.partial(open_body, pieces, sizes, slot_total),
        out_shape=(
            jax.ShapeDtypeStruct((spans, rows, half), f32),
            jax.ShapeDtypeStruct((spans, SUB, rows), f32),
            jax.ShapeDtypeStruct((2, modes, half), f32),
            jax.ShapeDtypeStruct((modes, half), f32),
            jax.ShapeDtypeStruct((modes, half), f32),
            pltpu.VMEM(weight.shape, weight.dtype),
        ),
        in_specs=[pl.BlockSpec(memory_space=pltpu.SMEM)] + [anywhere] * 7,
        out_specs=(vmem,) * 6,
        scratch_shapes=[
            pltpu.SMEM((spans, rows), jnp.int32),
            pltpu.SMEM((1,), jnp.int32),
            pltpu.VMEM((words, width), f32),
            pltpu.VMEM((rows, width), f32),
            pltpu.VMEM((slots, rows, half), f32),
            pltpu.VMEM((modes, width), f32),
            pltpu.SemaphoreType.DMA((pieces + 5,)),
            pltpu.SemaphoreType.DMA((half // sizes[0],)),
        ],
        compiler_params=params(10),
        cost_estimate=cost(2 * slots * rows * modes * half, 4 * words * width),
        name="open_step",
    )(
        meta, first, in_hbm(ids), in_hbm(table), in_hbm(cache), in_hbm(rates), in_hbm(resid),
        in_hbm(weight),
    )


def history_body(sizes, slot_total, meta, span_any, cache, rates_ref, resid_ref, weight, held_weight, *rest):
    del held_weight
    states, taps, weight_out = rest[:3]
    span_here, held_rows, sems, slot_sems = rest[3:]
    chunk, wide = sizes
    _, rows, half = held_rows.shape
    modes = rates_ref.shape[0]
    deep = early_rows(weight)
    later = weight.shape[0] - deep
    fetch = slot_fetch(1, chunk, meta, cache, held_rows, slot_sems)
    span_copy = pltpu.make_async_copy(span_any, span_here, sems.at[0])
    weight_copy = pltpu.make_async_copy(
        weight.at[pl.ds(deep, later), :], weight_out.at[pl.ds(deep, later), :], sems.at[1]
    )
    span_copy.start()
    for j in range(half // chunk):
        fetch(j).start()
    weight_copy.start()

    def tap_tile(t, carry):
        at = pl.ds(pl.multiple_of(t * LANES, LANES), LANES)
        rates, resid = rates_ref[:, at], resid_ref[:, at]
        place = lax.broadcasted_iota(jnp.int32, (SUB, LANES), 0).astype(f32)
        step8 = jnp.exp(-rates * float(SUB))
        first = [spread(resid, m) * jnp.exp(-spread(rates, m) * place) for m in range(modes)]

        def store(k, value):
            taps[k * SUB : (k + 1) * SUB, at] = value

        mode_rows(first, [spread(step8, m) for m in range(modes)], rows, store)
        return carry

    lax.fori_loop(0, half // LANES, tap_tile, 0)
    span_copy.wait()
    first_span = lax.rem(span_here[0], slot_total)
    half_states(
        0, wide, chunk // wide, slot_total, meta, first_span, fetch, held_rows, rates_ref, states
    )
    weight_copy.wait()


def history_states(meta, first, cache, rates, resid, weight, held_weight, slot_total):
    slots, rows, _ = cache.shape
    modes = rates.shape[0]
    half = weight.shape[1]
    sizes = tile_sizes(half)
    vmem, anywhere = pl.BlockSpec(memory_space=pltpu.VMEM), pl.BlockSpec(memory_space=pl.ANY)
    return pl.pallas_call(
        functools.partial(history_body, sizes, slot_total),
        out_shape=(
            jax.ShapeDtypeStruct((2, modes, half), f32),
            jax.ShapeDtypeStruct((rows, half), f32),
            pltpu.VMEM(weight.shape, weight.dtype),
        ),
        in_specs=[pl.BlockSpec(memory_space=pltpu.SMEM)]
        + [anywhere] * 2
        + [vmem] * 2
        + [anywhere] * 2,
        out_specs=(vmem,) * 3,
        scratch_shapes=[
            pltpu.SMEM((1,), jnp.int32),
            pltpu.VMEM((slots, rows, half), f32),
            pltpu.SemaphoreType.DMA((2,)),
            pltpu.SemaphoreType.DMA((half // sizes[0],)),
        ],
        input_output_aliases={6: 2},
        compiler_params=params(6),
        cost_estimate=cost(2 * slots * rows * modes * half, 4 * slots * rows * half),
        name="history_states",
    )(
        meta, first, in_hbm(cache), rates, resid, in_hbm(weight), in_vmem(held_weight),
    )


def gate_body(channels, span, counts, meta, base, *rest):
    n_delta, n_first, n_later, n_before, n_past, n_out, n_keep = counts
    rest = list(rest)

    def take(n):
        return [rest.pop(0) for _ in range(n)]

    delta = take(n_delta)
    gain, rates_ref, resid_ref, taps, mine, theirs = take(6)
    take(1)
    first_sums, later_sums, before = take(n_first), take(n_later), take(n_before)
    past = take(n_past)
    gated = rest.pop(0)
    normed_out, past_out = take(n_out), take(n_keep)
    padded, state_buf = rest
    rows, half = gated.shape
    modes = rates_ref.shape[0]
    blocks = rows // SUB
    is_first = meta[1] == 1
    wide = 4 * LANES if half % (4 * LANES) == 0 else LANES

    if n_before:

        def chain(t, carry):
            at = pl.ds(pl.multiple_of(t * wide, LANES), wide)
            decay = jnp.exp(-rates_ref[:, at])
            groups = [decay[g : g + SUB, :] for g in range(0, modes, SUB)]
            held = [jnp.zeros((SUB, wide), f32) for _ in groups]
            for r in range(rows):
                row = row_spread(before[0], r, at)
                held = [h * d + row for h, d in zip(held, groups)]
            state_buf[:, at] = jnp.concatenate(held, axis=0) * decay + (
                mine[span, :, at] + theirs[span, :, at]
            )
            return carry

        lax.fori_loop(0, half // wide, chain, 0)
    elif not n_past:
        state_buf[...] = mine[span] + theirs[span]

    sums = first_sums[0][span, 0:1, :]
    for ref in first_sums[1:]:
        sums = sums + ref[span, 0:1, :]
    if n_later:
        later = later_sums[0][span, 0:1, :]
        for ref in later_sums[1:]:
            later = later + ref[span, 0:1, :]
        sums = jnp.where(is_first, sums, later)
    here = lax.broadcasted_iota(jnp.int32, (rows, rows), 0)
    there = lax.broadcasted_iota(jnp.int32, (rows, rows), 1)
    column = jnp.sum(
        jnp.where(here == there, jnp.broadcast_to(sums, (rows, rows)), 0.0), axis=1, keepdims=True
    )
    scale = jnp.broadcast_to(lax.rsqrt(column / float(channels) + epsilon), (rows, LANES))
    padded[0:SUB, :] = jnp.zeros((SUB, LANES), f32)

    def tile(t, carry):
        at = pl.ds(pl.multiple_of(t * LANES, LANES), LANES)
        own = pl.ds(pl.multiple_of(meta[0] * half + t * LANES, LANES), LANES)
        current = base[span, :, at]
        if n_delta:
            current = current + jnp.where(is_first, 0.0, delta[0][:, at].astype(f32))
        normed = current * scale * gain[:, own]
        padded[SUB:, :] = normed
        if n_out:
            normed_out[0][:, at] = normed
        rates = rates_ref[:, at]
        total = [None] * blocks

        def store(k, value):
            total[k] = value

        if n_past:
            for k in range(blocks):
                total[k] = past[0][k * SUB : (k + 1) * SUB, at]
        else:
            weighted = resid_ref[:, at] * state_buf[:, at]
            step8 = jnp.exp(-rates * float(SUB))
            place = lax.broadcasted_iota(jnp.int32, (SUB, LANES), 0).astype(f32)
            first = [spread(weighted, m) * jnp.exp(-spread(rates, m) * place) for m in range(modes)]
            mode_rows(first, [spread(step8, m) for m in range(modes)], rows, store)
            if n_keep:
                for k in range(blocks):
                    past_out[0][k * SUB : (k + 1) * SUB, at] = total[k]
        for b in range(SUB):
            shifted = [
                padded[SUB + k * SUB - b : 2 * SUB + k * SUB - b, :] for k in range(blocks)
            ]
            for a in range(blocks):
                tap = row_spread(taps, a * SUB + b, at)
                for k in range(a, blocks):
                    total[k] = total[k] + tap * shifted[k - a]
        for k in range(blocks):
            block = padded[pl.ds(SUB + k * SUB, SUB), :]
            gated[k * SUB : (k + 1) * SUB, at] = (block * total[k]).astype(gated.dtype)
        return carry

    lax.fori_loop(0, half // LANES, tile, 0)


def gate(meta, base, delta, gain, modes_here, taps, weight, first_sums, later_sums, states, before, past, keep, span):
    spans, rows, half = base.shape
    modes = modes_here[0].shape[0]
    vmem = pl.BlockSpec(memory_space=pltpu.VMEM)
    deltas = [] if delta is None else [delta]
    want = int(span + 1 < spans)
    head = [base, *deltas, gain, *modes_here, taps, *states]
    operands = [*head, in_vmem(weight), *first_sums, *later_sums, *before, *past]
    in_specs = [vmem] * len(operands)
    in_specs[len(head)] = pl.BlockSpec(memory_space=pl.ANY)
    counts = (len(deltas), len(first_sums), len(later_sums), len(before), len(past), want, int(keep))
    out_shape = [jax.ShapeDtypeStruct((rows, half), jnp.bfloat16)]
    if want:
        out_shape.append(jax.ShapeDtypeStruct((rows, half), f32))
    if keep:
        out_shape.append(jax.ShapeDtypeStruct((rows, half), f32))
    return pl.pallas_call(
        functools.partial(gate_body, weight.shape[0], span, counts),
        out_shape=tuple(out_shape),
        in_specs=[pl.BlockSpec(memory_space=pltpu.SMEM)] + in_specs,
        out_specs=tuple(vmem for _ in out_shape),
        scratch_shapes=[pltpu.VMEM((rows + SUB, LANES), f32), pltpu.VMEM((modes, half), f32)],
        compiler_params=params(2),
        cost_estimate=cost(rows * rows * half + 4 * modes * rows * half, 12 * rows * half),
        name="gate",
    )(meta, *operands)


def source_of(step, rank, count):
    place = jnp.where(lax.rem(rank, 2) == 1, (rank + 1) // 2, lax.rem(count - rank // 2, count))
    came = lax.rem(place - step + count, count)
    return jnp.where(came <= count // 2, jnp.maximum(2 * came - 1, 0), 2 * (count - came))


def mix_body(kind, chosen, counts, out_tile, step, own, meta, *refs):
    parts, n_acc, n_base, n_delta, n_done, seqs, tensors = counts
    refs = list(refs)

    def take(n):
        return [refs.pop(0) for _ in range(n)]

    pieces = [take(len(chosen)) for _ in range(parts)]
    (weight,) = take(1)
    acc_in, base, delta, done = take(n_acc), take(n_base), take(n_delta), take(n_done)
    rows, depth = pieces[0][0].shape
    out = weight.shape[1]
    if step is None:
        starts = [0] * parts
    else:
        source = source_of(step, meta[2], tensors) * seqs
        starts = [
            pl.multiple_of((source + (meta[0] if mine else seqs - 1 - meta[0])) * depth, depth)
            for mine in own
        ]
    span = chosen[0]
    squares = jnp.zeros((rows, LANES), f32)
    leaving = []
    if kind == "out":
        fresh_buf, sems = refs[1:]
        for i, ref in enumerate(done):
            leaving.append(pltpu.make_async_copy(ref, refs[0].at[0, i], sems.at[i]))
            leaving[-1].start()
    for n in range(out // out_tile):
        at = slice(n * out_tile, (n + 1) * out_tile)
        total = None
        for p in range(parts):
            lhs = jnp.concatenate([piece[...] for piece in pieces[p]], axis=0)
            more = jnp.dot(lhs, weight[pl.ds(starts[p], depth), at], preferred_element_type=f32)
            total = more if total is None else total + more
        if n_acc and acc_in[0].shape[0] == total.shape[0]:
            total = total + acc_in[0][:, at]
        elif n_acc:
            total = total + acc_in[0][span * rows : (span + 1) * rows, at]
        if kind == "part":
            refs[0][:, at] = total
            continue
        if n_delta:
            total = total + jnp.where(meta[1] == 1, 0.0, delta[0][:, at].astype(f32))
        fresh = base[0][span, :, at] + total
        if kind == "hop":
            refs[0][:, at] = total.astype(refs[0].dtype)
            squares = squares + lane_tiles_squared(fresh)
        elif kind == "done":
            refs[0][:, at] = fresh
        else:
            fresh_buf[:, at] = fresh
            leaving.append(
                pltpu.make_async_copy(
                    fresh_buf.at[:, at], refs[0].at[0, span, :, at], sems.at[len(done) + n]
                )
            )
            leaving[-1].start()
    for copy in leaving:
        copy.wait()
    if kind == "hop":
        for ref in done:
            refs[1][0:span] = ref[0:span]
        refs[1][span] = row_sums(squares)


def mix(kind, meta, step, own, pieces, chosen, weight, acc, base, delta, seqs, tensors, done=()):
    rows, depth = pieces[0][0].shape
    out = weight.shape[1]
    vmem = pl.BlockSpec(memory_space=pltpu.VMEM)
    accs = [] if acc is None else [acc]
    bases = [] if kind == "part" else [base]
    deltas = [] if kind == "part" or delta is None else [delta]
    flat = [piece for part in pieces for piece in part]
    operands = [*flat, in_vmem(weight), *accs, *bases, *deltas, *done]
    counts = (len(pieces), len(accs), len(bases), len(deltas), len(done), seqs, tensors)
    whole = jax.ShapeDtypeStruct((rows * len(chosen), out), f32)
    out_shape, out_specs = whole, vmem
    if kind == "hop":
        out_shape = (
            jax.ShapeDtypeStruct((rows, out), jnp.bfloat16),
            jax.ShapeDtypeStruct((base.shape[0], SUB, rows), f32),
        )
        out_specs = (vmem, vmem)
    elif kind == "out":
        out_shape = jax.ShapeDtypeStruct((1, len(done) + 1, rows, out), f32)
        out_specs = pl.BlockSpec(memory_space=pl.ANY)
    out_tile = 4 * LANES if out % (4 * LANES) == 0 else LANES
    scratch = []
    if kind == "out":
        scratch = [
            pltpu.VMEM((rows, out), f32),
            pltpu.SemaphoreType.DMA((len(done) + out // out_tile,)),
        ]
    return pl.pallas_call(
        functools.partial(mix_body, kind, chosen, counts, out_tile, step, own),
        out_shape=out_shape,
        in_specs=[pl.BlockSpec(memory_space=pltpu.SMEM)] + [vmem] * len(operands),
        out_specs=out_specs,
        scratch_shapes=scratch,
        compiler_params=params(8),
        cost_estimate=cost(
            2 * rows * len(chosen) * depth * out * len(pieces), 2 * depth * out * len(pieces)
        ),
    )(meta, *operands)


def ring_fits(tensors):
    return tensors in (2, 4, 8)


def ring_order(count):
    return list(range(0, 1)) + list(range(1, count, 2)) + list(range(2, count, 2))[::-1]


def local(token_ids, leading_span_index, embed_table, norm_gain, decay_rates, residues, history, mix_weight):
    section_rank = lax.axis_index("section")
    sections = lax.axis_size("section")
    seq_rank = lax.axis_index("seq")
    seqs = lax.axis_size("seq")
    tensor_rank = lax.axis_index("tensor")
    tensors = lax.axis_size("tensor")
    rates, resid, cache, weight = decay_rates[0], residues[0], history[0], mix_weight[0]
    spans, _ = token_ids.shape
    slots, _, _ = cache.shape
    slot_total = slots * seqs
    order = ring_order(tensors)

    def along_ring(value, shift):
        return lax.ppermute(
            value, "tensor", [(order[i], order[(i + shift) % tensors]) for i in range(tensors)]
        )

    def swapped(value):
        return lax.ppermute(value, "seq", [(i, seqs - 1 - i) for i in range(seqs)])

    def to_next(value):
        return lax.ppermute(value, "section", [(i, (i + 1) % sections) for i in range(sections)])

    def across(value, flip):
        return lax.ppermute(value, "tensor", [(i, i ^ flip) for i in range(tensors)])

    def to_next_across(value, flip):
        route = []
        for i in range(tensors):
            for s in range(sections):
                route.append((i * sections + s, (i ^ flip) * sections + (s + 1) % sections))
        return lax.ppermute(value, ("tensor", "section"), route)

    is_first = (section_rank == 0).astype(jnp.int32)
    meta = jnp.stack([seq_rank, is_first, tensor_rank]).astype(jnp.int32)

    base, sums, for_partner, *modes_here, held_weight = open_step(
        meta, leading_span_index, token_ids, embed_table, cache, rates, resid, weight, slot_total
    )
    small_ring = ring_fits(tensors)
    first_sums = [sums]
    if small_ring:
        for k in range(1, tensors):
            first_sums.append(along_ring(sums, k))
    else:
        first_sums = [lax.psum(sums, "tensor")]
    partner = swapped(for_partner)
    states, taps, weight = history_states(
        meta, leading_span_index, cache, *modes_here, weight, held_weight, slot_total
    )

    every = tuple(range(spans))
    deltas = [None] * spans
    later_sums = []
    past = []
    for stage in range(sections):
        last_stage = stage + 1 == sections
        gates = []
        before = []
        for span in every:
            got = gate(
                meta, base, deltas[span], norm_gain, modes_here, taps, weight, first_sums,
                later_sums, [states, partner], before, past if span == 0 else [],
                span == 0 and stage == 0 and not last_stage, span,
            )
            gates.append(got[0])
            before = list(got[1:2])
            if len(got) == 3:
                past = [got[2]]
        acc = None
        moving = list(gates)
        results = []
        steps = tensors if small_ring else 1
        for k in range(steps):
            final = k + 1 == steps
            if small_ring:
                step = k
                crossed = []
                for span in every:
                    crossed.append(swapped(moving[span]))
                pairs = [list(moving), crossed]
                if not final:
                    for span in every:
                        moving[span] = along_ring(moving[span], 1)
            else:
                step = None
                pairs = [[lax.all_gather(g, ("tensor", "seq"), axis=1, tiled=True) for g in gates]]
            if not final:
                acc = mix(
                    "part", meta, step, (True, False), pairs, every, weight, acc, None, None,
                    seqs, tensors,
                )
                continue
            for span in every:
                kind = "hop" if not last_stage else "out" if span + 1 == spans else "done"
                done = ()
                if kind == "out":
                    done = tuple(results)
                elif kind == "hop" and span > 0:
                    done = (results[-1][1],)
                acc_here, rest = acc, [[part[span]] for part in pairs]
                own = (True, False)[: len(rest)]
                if small_ring:
                    acc_here = mix(
                        "part", meta, step, own[:1], rest[:1], (span,), weight, acc, None, None,
                        seqs, tensors,
                    )
                    own, rest = own[1:], rest[1:]
                results.append(
                    mix(
                        kind, meta, step, own, rest, (span,), weight, acc_here, base,
                        deltas[span], seqs, tensors, done,
                    )
                )
        if not last_stage:
            deltas = []
            for span in every:
                deltas.append(to_next(results[span][0]))
            both = results[-1][1]
            both = both + swapped(both)
            if small_ring:
                for bit in range(tensors.bit_length() - 2):
                    both = both + across(both, 1 << bit)
                later_sums = []
                for k in range(2):
                    later_sums.append(to_next_across(both, k * tensors // 2))
            else:
                later_sums = [to_next(lax.psum(both, "tensor"))]
    return results[-1]


def solution(mesh):
    placed = (
        P("groups", None),
        P("groups"),
        P(None, "tensor"),
        P("section", "tensor"),
        P("section", None, "tensor"),
        P("section", None, "tensor"),
        P("section", "seq", "groups", "tensor"),
        P("section", None, ("tensor", "seq")),
    )
    return jax.shard_map(
        local,
        mesh=mesh,
        in_specs=placed,
        out_specs=P("section", None, "groups", ("tensor", "seq")),
        check_vma=False,
    )
```
